256 devices in a mesh: table: 16 (over y, x), blk: 16 (over z, core).
Axes of the slice: x: 4, y: 4, z: 8, core: 2. Of those that a mesh axis runs over, the one named last changes fastest.
Arguments:
- cold_table: bfloat16 [524288, 128], P('table'), may hold values from -6 to 6
- slot_row: int32 [4096, 2048], P(('table', 'blk')), may hold values from 0 to 32767
- slot_sample: int32 [4096, 2048], P(('table', 'blk')), may hold values from 0 to 511
- slot_count: int32 [4096, 2048], P(('table', 'blk')), may hold values from 0 to 15, as said below
- hot_table: bfloat16 [4096, 128], replicated, may hold values from -6 to 6
- hot_index: int32 [131072, 8], P(('table', 'blk')), may hold values from 0 to 4095
- hot_count: int32 [131072, 8], P(('table', 'blk')), may hold values from 1 to 15
- hot_cotangent: bfloat16 [131072, 128], P(('table', 'blk')), may hold values from -0.59765625 to 0.59765625
Outputs:
- features: bfloat16 [131072, 256], P(('table', 'blk'))
- hot_grad: float32 [4096, 128], P('blk')
The draws below stay inside these ranges and needn't reach their ends.
Inputs may be any that keep to these rules, and one draw needn't show every extreme that they name: `slot_count`: slots of a bucket that carry no request have count 0 and follow its used slots; in every draw, for every index of blk, one cold shard receives 2048 used slots from every device with that index.
All inputs are finite; a program needn't handle non-finite values.
Results may differ from the reference program's by a relative error of at most 0.001.
Values may be sent and summed in bfloat16 or wider, within the bound.
No kernel may reach another device: no remote copies, remote signals or barrier semaphores. Data moves between devices by JAX's collectives and lax.ppermute only.
A program may use at most 128 MiB of HBM per device.

```python
import math
import jax
import jax.numpy as jnp
import numpy as np
from jax import lax

E = 128
S_DEV = 512
V_SHARD = 32768
KH = 8
CAP = 2048
PEERS = 16
REPLICAS = 16
BUCKETS = 4096
SAMPLES = 131072
VROWS = 524288
HOT = 4096


def slot_law(key):
    base_key = jax.random.fold_in(key, 7)
    key_owner, key_load, key_row, key_sample, key_count = jax.random.split(base_key, 5)
    bucket = jnp.arange(BUCKETS, dtype=jnp.int32)
    source = bucket // PEERS
    owner = bucket % PEERS
    busiest = jax.random.randint(key_owner, (REPLICAS,), 0, PEERS)
    is_busy = busiest[source % REPLICAS] == owner
    loads = jax.random.randint(key_load, (BUCKETS,), CAP // 8, CAP // 2 + 1)
    used = jnp.where(is_busy, CAP, loads)
    live = jnp.arange(CAP, dtype=jnp.int32)[None, :] < used[:, None]
    rows_drawn = jax.random.randint(key_row, (BUCKETS, CAP), 0, V_SHARD)
    samples_drawn = jax.random.randint(key_sample, (BUCKETS, CAP), 0, S_DEV)
    counts_drawn = jnp.where(live, jax.random.randint(key_count, (BUCKETS, CAP), 1, 16), 0)
    return (rows_drawn, samples_drawn, counts_drawn)


def draw_slot_row(key, part):
    return slot_law(key)[0]


def draw_slot_sample(key, part):
    return slot_law(key)[1]


def draw_slot_count(key, part):
    return slot_law(key)[2]


def place_ends(entries, key, least, largest):
    place = [jax.random.randint(jax.random.fold_in(key, axis), (), 0, length) for axis, length in enumerate(entries.shape)]
    widest = entries.shape.index(max(entries.shape))
    beside = place[:widest] + [(place[widest] + 1) % entries.shape[widest]] + place[widest + 1:]
    return entries.at[tuple(place)].set(least).at[tuple(beside)].set(largest)


def steps_of(rng, shape, shards, least, largest):
    gain, own = 1.0, jax.random.fold_in(rng, 6)
    for axis_at, shards_of in shards:
        draws = jnp.exp(jax.random.uniform(jax.random.fold_in(own, axis_at), (shards_of,), jnp.float32, least / len(shards), largest / len(shards)))
        gain = gain * jnp.repeat(draws, shape[axis_at] // shards_of).reshape([-1 if axis == axis_at else 1 for axis in range(len(shape))])
    return gain


def rank_bounds(number_of, skew):
    portions = [(1 << 20) // math.isqrt(grade ** skew) + 1 for grade in range(1, number_of + 1)]
    scale = 1 + sum(portions) // (1 << 30)
    return np.cumsum(np.array([max(1, weight // scale) for weight in portions]))


def ranked(own_key, extent, amount, lean):
    listing = rank_bounds(amount, lean)
    pick = jax.random.randint(jax.random.fold_in(own_key, 1), extent, 0, int(listing[amount - 1]))
    rank = jnp.searchsorted(jnp.asarray(listing, jnp.int32), pick, side="right")
    return jax.random.permutation(jax.random.fold_in(own_key, 2), amount)[rank].astype(jnp.int32)


def scatter_about(rng, dims, scale, reach, cuts=(), kind=jnp.bfloat16):
    values = scale * jax.random.normal(rng, dims, jnp.float32)
    if cuts:
        values = values * steps_of(rng, dims, cuts, -0.22, 0.18)
    return jnp.clip(values, -reach, reach).astype(kind)


def setup_inputs(seed: int = 0) -> dict:
    key_of = jax.random.split(jax.random.key(seed), 9)
    return {
        "cold_table": scatter_about(key_of[0], (VROWS, E), 1.0, 6.0, ((0, 16),)),
        "slot_row": draw_slot_row(jax.random.fold_in(key_of[8], 71), 0),
        "slot_sample": draw_slot_sample(jax.random.fold_in(key_of[8], 71), 0),
        "slot_count": draw_slot_count(jax.random.fold_in(key_of[8], 71), 0),
        "hot_table": scatter_about(key_of[4], (HOT, E), 1.0, 6.0),
        "hot_index": place_ends(ranked(key_of[5], (SAMPLES, KH), HOT, 1), jax.random.fold_in(key_of[5], 3), 0, HOT - 1).astype(jnp.int32),
        "hot_count": place_ends(jax.random.randint(key_of[6], (SAMPLES, KH), 1, 16), jax.random.fold_in(key_of[6], 1), 1, 15).astype(jnp.int32),
        "hot_cotangent": scatter_about(key_of[7], (SAMPLES, E), 0.1, 0.59765625, ((0, 256),)),
    }


cold_scale = 0.03125
hot_scale = 0.0625

def reference(cold_table, slot_row, slot_sample, slot_count, hot_table, hot_index, hot_count, hot_cotangent):
    sources = slot_row.shape[0] // PEERS
    owner_base = (jnp.arange(PEERS, dtype=jnp.int32) * V_SHARD)[:, None]

    def pool_cold(packed):
        local_rows, sample_idx, counts = packed
        picked = jnp.take(cold_table, (local_rows + owner_base).reshape(-1), axis=0).astype(jnp.float32)
        weights = counts.reshape(-1).astype(jnp.float32) * cold_scale
        return jax.ops.segment_sum(picked * weights[:, None], sample_idx.reshape(-1), num_segments=S_DEV)
    cold_pooled = lax.map(pool_cold, (slot_row.reshape(sources, PEERS, CAP), slot_sample.reshape(sources, PEERS, CAP), slot_count.reshape(sources, PEERS, CAP)))
    cold_pooled = cold_pooled.reshape(SAMPLES, E).astype(jnp.bfloat16)
    index_blocks = hot_index.reshape(sources, S_DEV, KH)
    count_blocks = hot_count.reshape(sources, S_DEV, KH)
    grad_blocks = hot_cotangent.reshape(sources, S_DEV, E)

    def pool_hot(packed):
        indices, counts = packed
        picked = jnp.take(hot_table, indices.reshape(-1), axis=0).astype(jnp.float32).reshape(S_DEV, KH, E)
        return lax.optimization_barrier(jnp.sum(picked * (counts.astype(jnp.float32) * hot_scale)[:, :, None], axis=1))
    hot_pooled = lax.map(pool_hot, (index_blocks, count_blocks)).reshape(SAMPLES, E).astype(jnp.bfloat16)

    def add_grad(total, packed):
        indices, counts, grads = packed
        weighted = grads.astype(jnp.float32)[:, None, :] * (counts.astype(jnp.float32) * hot_scale)[:, :, None]
        return (total + jax.ops.segment_sum(weighted.reshape(-1, E), indices.reshape(-1), num_segments=HOT), None)
    hot_grad, _ = lax.scan(add_grad, jnp.zeros((HOT, E), jnp.float32), (index_blocks, count_blocks, grad_blocks))
    features = jnp.concatenate([cold_pooled, hot_pooled], axis=1)
    return (features, hot_grad)
```

```python
import functools

import jax
import jax.numpy as jnp
from jax import lax
from jax.experimental import pallas as pl
from jax.experimental.pallas import tpu as pltpu
from jax.sharding import Mesh, PartitionSpec as P

cold_scale = 0.03125
hot_scale = 0.0625
CHUNK = 256
ALL = ("y", "x", "z", "core")


def widen_kernel(table_hbm, wide_ref, buf, sem):
    rows = buf.shape[1]
    steps = table_hbm.shape[0] // rows

    def fetch(step):
        return pltpu.make_async_copy(
            table_hbm.at[pl.ds(step * rows, rows)], buf.at[step % 2], sem.at[step % 2]
        )

    fetch(0).start()
    for step in range(steps):
        if step + 1 < steps:
            fetch(step + 1).start()
        fetch(step).wait()
        wide_ref[step * rows : (step + 1) * rows] = buf[step % 2].astype(jnp.float32)


def widen(table):
    rows, width = table.shape
    return pl.pallas_call(
        widen_kernel,
        in_specs=[pl.BlockSpec(memory_space=pl.ANY)],
        out_specs=pl.BlockSpec(memory_space=pltpu.VMEM),
        out_shape=pltpu.VMEM((rows, width), jnp.float32),
        scratch_shapes=[
            pltpu.VMEM((2, 2048, width), jnp.bfloat16),
            pltpu.SemaphoreType.DMA((2,)),
        ],
        compiler_params=pltpu.CompilerParams(vmem_limit_bytes=20 << 20),
        cost_estimate=pl.CostEstimate(
            flops=rows * width, bytes_accessed=rows * width * 6, transcendentals=0
        ),
        name="widen",
    )(table)


def pool_task(rows_ref, sample_ref, count_ref, wide_ref, acc, bufs):
    slots = rows_ref.shape[2]
    samples = acc.shape[0]

    def gather(chunk):
        buf = bufs[chunk % 2]
        for slot in range(CHUNK):
            row = rows_ref[0, 0, chunk * CHUNK + slot]
            buf[slot : slot + 1, :] = wide_ref[pl.ds(row, 1), :]

    def pool(chunk):
        cols = slice(chunk * CHUNK, (chunk + 1) * CHUNK)
        ids = lax.broadcasted_iota(jnp.int32, (samples, CHUNK), 0)
        weight = count_ref[0, :, cols].astype(jnp.float32) * cold_scale
        weights = jnp.where(ids == sample_ref[0, :, cols], weight, 0.0).astype(jnp.bfloat16)
        part = jnp.dot(
            weights,
            bufs[chunk % 2][...].astype(jnp.bfloat16),
            preferred_element_type=jnp.float32,
        )
        if chunk == 0:
            acc[...] = part
        else:
            acc[...] += part

    gather(0)
    for chunk in range(slots // CHUNK):
        if (chunk + 1) * CHUNK < slots:
            gather(chunk + 1)
        pool(chunk)


def far_kernel(order, rows_ref, sample_ref, count_ref, wide_ref, *refs):
    del order
    outs, (acc, buf0, buf1) = refs[:6], refs[6:]
    pool_task(rows_ref, sample_ref, count_ref, wide_ref, acc, (buf0, buf1))
    task = pl.program_id(0)
    half = acc.shape[0] // 2
    for i in range(3):

        @pl.when(task // 3 == i)
        def _():
            outs[i][0] = acc[:half]

        @pl.when(task % 3 == i)
        def _():
            outs[3 + i][0] = acc[half:]


def near_kernel(order, rows_ref, sample_ref, count_ref, wide_ref, out, acc, buf0, buf1):
    del order
    pool_task(rows_ref, sample_ref, count_ref, wide_ref, acc, (buf0, buf1))
    out[0] = acc[...]


def request_specs(slots):
    def spec(part, space):
        return pl.BlockSpec(
            (1, 1, slots), lambda t, order: (3 * order[t] + part, 0, 0), memory_space=space
        )

    return [
        spec(0, pltpu.SMEM),
        spec(1, pltpu.VMEM),
        spec(2, pltpu.VMEM),
        pl.BlockSpec(memory_space=pltpu.VMEM),
    ]


def pool_call(body, name, order, requests, wide, samples, out_specs, out_shape):
    slots = requests.shape[2]
    width = wide.shape[1]
    tasks = order.shape[0]
    return pl.pallas_call(
        body,
        grid_spec=pltpu.PrefetchScalarGridSpec(
            num_scalar_prefetch=1,
            grid=(tasks,),
            in_specs=request_specs(slots),
            out_specs=out_specs,
            scratch_shapes=[pltpu.VMEM((samples, width), jnp.float32)]
            + [pltpu.VMEM((CHUNK, width), jnp.float32)] * 2,
        ),
        out_shape=out_shape,
        compiler_params=pltpu.CompilerParams(vmem_limit_bytes=20 << 20),
        cost_estimate=pl.CostEstimate(
            flops=tasks * 2 * samples * slots * width,
            bytes_accessed=tasks * slots * width * 20,
            transcendentals=0,
        ),
        name=name,
    )(order, requests, requests, requests, wide)


def pool_far(order, requests, wide, samples):
    width = wide.shape[1]
    half = samples // 2
    specs = [
        pl.BlockSpec(
            (1, half, width), lambda t, order, i=i: (jnp.clip(t - 3 * i, 0, 2), 0, 0)
        )
        for i in range(3)
    ] + [
        pl.BlockSpec(
            (1, half, width),
            lambda t, order, i=i: (jnp.clip((t - i + 3) // 3 - 1, 0, 2), 0, 0),
        )
        for i in range(3)
    ]
    shape = [jax.ShapeDtypeStruct((3, half, width), jnp.float32)] * 6
    return pool_call(far_kernel, "pool_far", order, requests, wide, samples, specs, shape)


def pool_near(order, requests, wide, samples):
    width = wide.shape[1]
    return pool_call(
        near_kernel,
        "pool_near",
        order,
        requests,
        wide,
        samples,
        pl.BlockSpec((1, samples, width), lambda t, order: (t, 0, 0)),
        jax.ShapeDtypeStruct((order.shape[0], samples, width), jnp.float32),
    )


def relay_kernel(near_ref, *refs):
    got, outs = refs[:6], refs[6:]
    half = got[0].shape[1]
    for i in range(3):
        outs[i][:half] = near_ref[i, :half] + (got[0][i] + got[1][i] + got[2][i])
        outs[i][half:] = near_ref[i, half:]
        outs[3 + i][:half] = near_ref[3 + i, :half]
        outs[3 + i][half:] = near_ref[3 + i, half:] + (got[3][i] + got[4][i] + got[5][i])


def relay(near, got):
    _, samples, width = near.shape
    return pl.pallas_call(
        relay_kernel,
        out_shape=[jax.ShapeDtypeStruct((samples, width), jnp.float32)] * 6,
        compiler_params=pltpu.CompilerParams(vmem_limit_bytes=16 << 20),
        cost_estimate=pl.CostEstimate(
            flops=samples * width * 12, bytes_accessed=samples * width * 84, transcendentals=0
        ),
        name="relay",
    )(near, *got)


def finish_kernel(near_ref, a, b, c, d, e, f, hot_own, hot_got, out):
    width = a.shape[1]
    cold = near_ref[0] + ((a[...] + b[...] + c[...]) + (d[...] + e[...] + f[...]))
    out[:, :width] = cold.astype(jnp.bfloat16)
    out[:, width:] = (hot_own[...] + hot_got[...]).astype(jnp.bfloat16)


def finish(near, got, hot_own, hot_got):
    _, samples, width = near.shape
    whole = pl.BlockSpec((samples, width), lambda i: (0, 0))
    return pl.pallas_call(
        finish_kernel,
        grid=(1,),
        in_specs=[pl.BlockSpec((1, samples, width), lambda i: (6, 0, 0))] + [whole] * 8,
        out_specs=pl.BlockSpec((samples, 2 * width), lambda i: (0, 0)),
        out_shape=jax.ShapeDtypeStruct((samples, 2 * width), jnp.bfloat16),
        compiler_params=pltpu.CompilerParams(vmem_limit_bytes=16 << 20),
        cost_estimate=pl.CostEstimate(
            flops=samples * width * 8, bytes_accessed=samples * width * 40, transcendentals=0
        ),
        name="finish",
    )(near, *got, hot_own, hot_got)


def hot_kernel(core_ref, idx_ref, cnt_ref, cot_ref, table_ref, grad_ref, pool_ref, inc, pooled):
    block = table_ref.shape[1]
    lookups, samples = idx_ref.shape
    lanes = 128
    tile = 16
    core = core_ref[0]

    def step(z, carry):
        start = (2 * z + core) * block
        for lane in range(samples // lanes):
            cols = slice(lane * lanes, (lane + 1) * lanes)
            local = jnp.clip(idx_ref[:, cols] - start, -1, block)
            weight = cnt_ref[:, cols].astype(jnp.float32) * hot_scale
            keys = []
            for k in range(lookups):
                keys.append(
                    (
                        jnp.broadcast_to(local[k : k + 1], (tile, lanes)).astype(jnp.int16),
                        jnp.broadcast_to(weight[k : k + 1], (tile, lanes)).astype(jnp.bfloat16),
                    )
                )
            base = lax.broadcasted_iota(jnp.int32, (tile, lanes), 0)
            for group in range(block // tile):
                ids = (base + group * tile).astype(jnp.int16)
                total = jnp.zeros((tile, lanes), jnp.bfloat16)
                for key, value in keys:
                    total = total + jnp.where(ids == key, value, jnp.bfloat16(0))
                inc[group * tile : (group + 1) * tile, cols] = total
        grad_ref[z] = jnp.dot(inc[...], cot_ref[...], preferred_element_type=jnp.float32)
        part = lax.dot_general(
            table_ref[2 * z + core],
            inc[...],
            (((0,), (0,)), ((), ())),
            preferred_element_type=jnp.float32,
        )

        @pl.when(z == 0)
        def _():
            pooled[...] = part

        @pl.when(z > 0)
        def _():
            pooled[...] += part

        return carry

    lax.fori_loop(0, grad_ref.shape[0], step, 0)
    pool_ref[...] = jnp.transpose(pooled[...])


def hot_call(core, idx, cnt, cot, table, depth):
    blocks, block, width = table.shape
    samples = idx.shape[1]
    vmem = pl.BlockSpec(memory_space=pltpu.VMEM)
    return pl.pallas_call(
        hot_kernel,
        in_specs=[pl.BlockSpec(memory_space=pltpu.SMEM), vmem, vmem, vmem, vmem],
        out_specs=[vmem, vmem],
        out_shape=[
            jax.ShapeDtypeStruct((depth, block, width), jnp.float32),
            jax.ShapeDtypeStruct((samples, width), jnp.float32),
        ],
        scratch_shapes=[
            pltpu.VMEM((block, samples), jnp.bfloat16),
            pltpu.VMEM((width, samples), jnp.float32),
        ],
        compiler_params=pltpu.CompilerParams(vmem_limit_bytes=16 << 20),
        cost_estimate=pl.CostEstimate(
            flops=4 * samples * depth * block * width,
            bytes_accessed=samples * depth * block * 16,
            transcendentals=0,
        ),
        name="hot",
    )(core, idx, cnt, cot, table)


def shift(axis, size, by, value):
    return lax.ppermute(value, axis, [(i, (i + by) % size) for i in range(size)])


def shards(
    cold_table, slot_row, slot_sample, slot_count, hot_table, hot_index, hot_count, hot_cotangent
):
    samples = hot_index.shape[0]
    width = cold_table.shape[1]
    peers, slots = slot_row.shape
    side = lax.axis_size("x")
    depth = lax.axis_size("z")
    y, x, core = lax.axis_index("y"), lax.axis_index("x"), lax.axis_index("core")

    asked = jnp.stack([slot_row, slot_sample, slot_count], axis=1).reshape(3 * peers, 1, slots)
    requests = lax.all_to_all(asked, ("y", "x"), split_axis=0, concat_axis=0, tiled=True)
    wide = widen(cold_table)

    index_t, count_t = hot_index.T, hot_count.T
    idx = jnp.concatenate([index_t, shift("core", 2, 1, index_t)], axis=1)
    cnt = jnp.concatenate([count_t, shift("core", 2, 1, count_t)], axis=1)
    cot = jnp.concatenate([hot_cotangent, shift("core", 2, 1, hot_cotangent)], axis=0)
    blocks = hot_table.reshape(2 * depth, -1, width)
    grad, pooled = hot_call(core.reshape(1), idx, cnt, cot, blocks, depth)
    hot_own = pooled[:samples]
    hot_got = shift("core", 2, 1, pooled[samples:])
    grad = lax.all_to_all(grad, "z", split_axis=0, concat_axis=0, tiled=True)

    def source(dy, dx):
        return ((y + dy) % side) * side + (x + dx) % side

    far = jnp.stack([source(dy, dx) for dx in (1, 2, 3) for dy in (1, 2, 3)])
    near = jnp.stack(
        [source(dy, 0) for dy in (1, 2, 3)]
        + [source(0, dx) for dx in (1, 2, 3)]
        + [source(0, 0)]
    )
    sent = pool_far(far.astype(jnp.int32), requests, wide, samples)
    got = [shift("x", side, i + 1, sent[i]) for i in range(3)] + [
        shift("y", side, i + 1, sent[3 + i]) for i in range(3)
    ]
    close = pool_near(near.astype(jnp.int32), requests, wide, samples)
    passed = relay(close, got)
    last = [shift("y", side, i + 1, passed[i]) for i in range(3)] + [
        shift("x", side, i + 1, passed[3 + i]) for i in range(3)
    ]
    features = finish(close, last, hot_own, hot_got)

    share = jnp.sum(grad, axis=0)
    for axis in ("x", "y"):
        one, two, three = (shift(axis, side, by, share) for by in (1, 2, 3))
        share = (share + two) + (one + three)
    return (features, share)


def solution(mesh):
    fine = Mesh(mesh.devices.reshape(4, 4, 8, 2), ALL)
    every = P(ALL, None)
    return jax.shard_map(
        shards,
        mesh=fine,
        in_specs=(P(("y", "x"), None), every, every, every, P(), every, every, every),
        out_specs=(every, P(("z", "core"), None)),
        check_vma=False,
    )
```

```python
import functools

import jax
import jax.numpy as jnp
from jax import lax
from jax.experimental import pallas as pl
from jax.experimental.pallas import tpu as pltpu
from jax.sharding import Mesh, PartitionSpec as P

cold_scale = 0.03125
hot_scale = 0.0625
CHUNK = 256
ALL = ("y", "x", "z", "core")


def widen_kernel(table_hbm, wide_ref, buf, sem):
    steps = sem.shape[0]
    rows = buf.shape[0] // steps

    def fetch(step):
        part = pl.ds(step * rows, rows)
        return pltpu.make_async_copy(table_hbm.at[part], buf.at[part], sem.at[step])

    for step in range(steps):
        fetch(step).start()
    for step in range(steps):
        fetch(step).wait()
        part = slice(step * rows, (step + 1) * rows)
        wide_ref[part] = buf[part].astype(jnp.float32)


def widen(table):
    rows, width = table.shape
    return pl.pallas_call(
        widen_kernel,
        in_specs=[pl.BlockSpec(memory_space=pl.ANY)],
        out_specs=pl.BlockSpec(memory_space=pltpu.VMEM),
        out_shape=pltpu.VMEM((rows, width), jnp.float32),
        scratch_shapes=[
            pltpu.VMEM((rows, width), jnp.bfloat16),
            pltpu.SemaphoreType.DMA((16,)),
        ],
        compiler_params=pltpu.CompilerParams(vmem_limit_bytes=44 << 20),
        cost_estimate=pl.CostEstimate(
            flops=rows * width, bytes_accessed=rows * width * 6, transcendentals=0
        ),
        name="widen",
    )(table)


def pack_kernel(a, b, c, out):
    for part, ref in enumerate((a, b, c)):
        for bucket in range(ref.shape[0]):
            out[bucket, part : part + 1, :] = ref[bucket : bucket + 1, :]


def pack(parts):
    buckets, slots = parts[0].shape
    return pl.pallas_call(
        pack_kernel,
        grid=(1,),
        in_specs=[pl.BlockSpec((buckets, slots), lambda i: (0, 0))] * 3,
        out_specs=pl.BlockSpec((buckets, 3, slots), lambda i: (0, 0, 0)),
        out_shape=jax.ShapeDtypeStruct((buckets, 3, slots), jnp.int32),
        compiler_params=pltpu.CompilerParams(vmem_limit_bytes=60 << 20),
        cost_estimate=pl.CostEstimate(
            flops=0, bytes_accessed=buckets * slots * 24, transcendentals=0
        ),
        name="pack",
    )(*parts)


def pool_task(rows_ref, slots_ref, wide_ref, acc, bufs):
    slots = rows_ref.shape[2]
    samples = acc.shape[0]

    def gather(chunk):
        buf = bufs[chunk % 2]
        for slot in range(CHUNK):
            row = rows_ref[0, 0, chunk * CHUNK + slot]
            buf[slot : slot + 1, :] = wide_ref[pl.ds(row, 1), :]

    def pool(chunk):
        cols = slice(chunk * CHUNK, (chunk + 1) * CHUNK)
        ids = lax.broadcasted_iota(jnp.int32, (samples, CHUNK), 0)
        weight = slots_ref[0, 2:3, cols].astype(jnp.float32) * cold_scale
        weights = jnp.where(ids == slots_ref[0, 1:2, cols], weight, 0.0).astype(jnp.bfloat16)
        part = jnp.dot(
            weights,
            bufs[chunk % 2][...].astype(jnp.bfloat16),
            preferred_element_type=jnp.float32,
        )
        if chunk == 0:
            acc[...] = part
        else:
            acc[...] += part

    gather(0)
    for chunk in range(slots // CHUNK):
        if (chunk + 1) * CHUNK < slots:
            gather(chunk + 1)
        pool(chunk)


def far_kernel(place, rows_ref, slots_ref, wide_ref, *refs):
    del place
    outs, (acc, buf0, buf1) = refs[:6], refs[6:]
    pool_task(rows_ref, slots_ref, wide_ref, acc, (buf0, buf1))
    task = pl.program_id(0)
    half = acc.shape[0] // 2
    part = half // 2
    for i in range(3):

        @pl.when(task // 3 == i)
        def _():
            outs[i][0] = acc[:part]
            outs[i][1] = acc[part:half]

        @pl.when(task % 3 == i)
        def _():
            outs[3 + i][0] = acc[half : half + part]
            outs[3 + i][1] = acc[half + part :]


def near_kernel(place, rows_ref, slots_ref, wide_ref, out, acc, buf0, buf1):
    del place
    pool_task(rows_ref, slots_ref, wide_ref, acc, (buf0, buf1))
    out[0] = acc[...]


def source(place, dy, dx):
    return ((place[2] + dy) & 3) * 4 + ((place[3] + dx) & 3)


def far_source(t, place):
    return source(place, t % 3 + 1, t // 3 + 1)


def near_source(t, place):
    return source(place, jnp.where(t < 3, t + 1, 0), jnp.where(t < 3, 0, t - 2))


def own_source(t, place):
    return source(place, 0, 0)


def pool_call(body, name, origin, tasks, place, requests, wide, samples, out_specs, out_shape):
    _, parts, slots = requests.shape
    width = wide.shape[1]

    def spec(space):
        return pl.BlockSpec(
            (1, parts, slots), lambda t, place: (origin(t, place), 0, 0), memory_space=space
        )

    return pl.pallas_call(
        body,
        grid_spec=pltpu.PrefetchScalarGridSpec(
            num_scalar_prefetch=1,
            grid=(tasks,),
            in_specs=[spec(pltpu.SMEM), spec(pltpu.VMEM), pl.BlockSpec(memory_space=pltpu.VMEM)],
            out_specs=out_specs,
            scratch_shapes=[pltpu.VMEM((samples, width), jnp.float32)]
            + [pltpu.VMEM((CHUNK, width), jnp.float32)] * 2,
        ),
        out_shape=out_shape,
        compiler_params=pltpu.CompilerParams(vmem_limit_bytes=20 << 20),
        cost_estimate=pl.CostEstimate(
            flops=tasks * 2 * samples * slots * width,
            bytes_accessed=tasks * slots * width * 20,
            transcendentals=0,
        ),
        name=name,
    )(place, requests, requests, wide)


def pool_far(place, requests, wide, samples):
    width = wide.shape[1]
    part = samples // 4
    specs = [
        pl.BlockSpec(
            (2, part, width), lambda t, place, i=i: (jnp.clip(t - 3 * i, 0, 2), 0, 0)
        )
        for i in range(3)
    ] + [
        pl.BlockSpec(
            (2, part, width),
            lambda t, place, i=i: (jnp.clip((t - i + 3) // 3 - 1, 0, 2), 0, 0),
        )
        for i in range(3)
    ]
    shape = [jax.ShapeDtypeStruct((7, part, width), jnp.float32)] * 6
    return pool_call(
        far_kernel, "pool_far", far_source, 9, place, requests, wide, samples, specs, shape
    )


def pool_near(name, origin, tasks, place, requests, wide, samples):
    width = wide.shape[1]
    return pool_call(
        near_kernel,
        name,
        origin,
        tasks,
        place,
        requests,
        wide,
        samples,
        pl.BlockSpec((1, samples, width), lambda t, place: (t, 0, 0)),
        jax.ShapeDtypeStruct((tasks, samples, width), jnp.float32),
    )


def attach_kernel(*refs):
    parts, outs, share_ref = refs[:8], refs[14:20], refs[20]
    p = [ref[...] for ref in parts]
    share = ((p[0] + p[1]) + (p[2] + p[3])) + ((p[4] + p[5]) + (p[6] + p[7]))
    share_ref[...] = share
    half = share.shape[0] // 2
    for out in outs[:3]:
        out[0] = share[:half]
    for out in outs[3:]:
        out[0] = share[half:]


def attach(parts, sent):
    block, width = parts[0].shape
    last = pl.BlockSpec((1, block // 2, width), lambda i: (6, 0, 0))
    whole = pl.BlockSpec((block, width), lambda i: (0, 0))
    return pl.pallas_call(
        attach_kernel,
        grid=(1,),
        in_specs=[whole] * 8 + [pl.BlockSpec(memory_space=pl.ANY)] * 6,
        out_specs=[last] * 6 + [whole],
        out_shape=[jax.ShapeDtypeStruct(sent[0].shape, jnp.float32)] * 6
        + [jax.ShapeDtypeStruct((block, width), jnp.float32)],
        input_output_aliases={8 + i: i for i in range(6)},
        compiler_params=pltpu.CompilerParams(vmem_limit_bytes=8 << 20),
        cost_estimate=pl.CostEstimate(
            flops=block * width * 8, bytes_accessed=block * width * 48, transcendentals=0
        ),
        name="attach",
    )(*parts, *sent)


def relay_kernel(near_ref, share_ref, *refs):
    got, outs = refs[:6], refs[6:]
    samples = near_ref.shape[1]
    half = samples // 2
    part = half // 2
    for s, (way, rows) in enumerate(((got[:3], slice(0, part)), (got[3:], slice(part, half)))):
        one, two, three = way
        share = (share_ref[rows] + two[6]) + (one[6] + three[6])
        for i in range(3):
            near, out = near_ref.at[3 * s + i], outs[3 * s + i]
            direct = slice(half, samples) if s == 0 else slice(0, half)
            out[direct] = near[direct]
            out[samples:] = share
            for q in range(2):
                at = slice(s * half + q * part, s * half + (q + 1) * part)
                out[at] = near[at] + (one[2 * i + q] + two[2 * i + q] + three[2 * i + q])


def relay(near, share, got):
    _, samples, width = near.shape
    tall = samples + share.shape[0] // 2
    return pl.pallas_call(
        relay_kernel,
        out_shape=[jax.ShapeDtypeStruct((tall, width), jnp.float32)] * 6,
        compiler_params=pltpu.CompilerParams(vmem_limit_bytes=16 << 20),
        cost_estimate=pl.CostEstimate(
            flops=samples * width * 12, bytes_accessed=samples * width * 84, transcendentals=0
        ),
        name="relay",
    )(near, share, *got)


def finish_kernel(near_ref, mine0, mine1, a, b, c, d, e, f, hot_own, hot_got, out, grad):
    samples, width = hot_own.shape
    half = grad.shape[0] // 2
    cold = near_ref[0] + (
        (a[:samples] + b[:samples] + c[:samples]) + (d[:samples] + e[:samples] + f[:samples])
    )
    out[:, :width] = cold.astype(jnp.bfloat16)
    out[:, width:] = (hot_own[...] + hot_got[...]).astype(jnp.bfloat16)
    grad[:half] = (mine0[samples:] + b[samples:]) + (a[samples:] + c[samples:])
    grad[half:] = (mine1[samples:] + e[samples:]) + (d[samples:] + f[samples:])


def finish(near, mine0, mine1, got, hot_own, hot_got):
    _, samples, width = near.shape
    tall = mine0.shape[0]
    whole = pl.BlockSpec((samples, width), lambda i: (0, 0))
    more = pl.BlockSpec((tall, width), lambda i: (0, 0))
    share = 2 * (tall - samples)
    return pl.pallas_call(
        finish_kernel,
        grid=(1,),
        in_specs=[pl.BlockSpec((1, samples, width), lambda i: (0, 0, 0))]
        + [more] * 8
        + [whole] * 2,
        out_specs=[
            pl.BlockSpec((samples, 2 * width), lambda i: (0, 0)),
            pl.BlockSpec((share, width), lambda i: (0, 0)),
        ],
        out_shape=[
            jax.ShapeDtypeStruct((samples, 2 * width), jnp.bfloat16),
            jax.ShapeDtypeStruct((share, width), jnp.float32),
        ],
        compiler_params=pltpu.CompilerParams(vmem_limit_bytes=16 << 20),
        cost_estimate=pl.CostEstimate(
            flops=samples * width * 8, bytes_accessed=samples * width * 40, transcendentals=0
        ),
        name="finish",
    )(near, mine0, mine1, *got, hot_own, hot_got)


def hot_kernel(place, idx0, idx1, cnt0, cnt1, cot0, cot1, table_ref, *refs):
    grads, (own_ref, other_ref, inc, pooled, held) = refs[:8], refs[8:]
    block = table_ref.shape[1]
    lookups, samples = idx0.shape
    depth = held.shape[0]
    lanes = 128
    tile = 16

    def step(ahead, carry):
        blk = 2 * lax.rem(place[0] + ahead, depth) + place[1]
        start = blk * block
        for lane in range(2 * samples // lanes):
            idx_ref, cnt_ref = (idx0, cnt0) if lane * lanes < samples else (idx1, cnt1)
            first = lane * lanes % samples
            cols = slice(first, first + lanes)
            to = slice(lane * lanes, (lane + 1) * lanes)
            local = jnp.clip(idx_ref[:, cols] - start, -1, block)
            weight = cnt_ref[:, cols].astype(jnp.float32) * hot_scale
            keys = []
            for k in range(lookups):
                keys.append(
                    (
                        jnp.broadcast_to(local[k : k + 1], (tile, lanes)).astype(jnp.int16),
                        jnp.broadcast_to(weight[k : k + 1], (tile, lanes)).astype(jnp.bfloat16),
                    )
                )
            base = lax.broadcasted_iota(jnp.int32, (tile, lanes), 0)
            for group in range(block // tile):
                ids = (base + group * tile).astype(jnp.int16)
                total = jnp.zeros((tile, lanes), jnp.bfloat16)
                for key, value in keys:
                    total = total + jnp.where(ids == key, value, jnp.bfloat16(0))
                inc[group * tile : (group + 1) * tile, to] = total
        held[ahead] = jnp.dot(
            inc[:, :samples], cot0[...], preferred_element_type=jnp.float32
        ) + jnp.dot(inc[:, samples:], cot1[...], preferred_element_type=jnp.float32)
        part = lax.dot_general(
            table_ref[blk],
            inc[...],
            (((0,), (0,)), ((), ())),
            preferred_element_type=jnp.float32,
        )

        @pl.when(ahead == 0)
        def _():
            pooled[...] = part

        @pl.when(ahead > 0)
        def _():
            pooled[...] += part

        return carry

    lax.fori_loop(0, depth, step, 0)
    own_ref[...] = jnp.transpose(pooled[:, :samples])
    other_ref[...] = jnp.transpose(pooled[:, samples:])
    for ahead in range(depth):
        grads[ahead][...] = held[ahead]


def hot_call(place, pairs, table, depth):
    blocks, block, width = table.shape
    lookups, samples = pairs[0].shape

    def whole(*shape):
        return pl.BlockSpec(shape, lambda i, place: (0,) * len(shape))

    return pl.pallas_call(
        hot_kernel,
        grid_spec=pltpu.PrefetchScalarGridSpec(
            num_scalar_prefetch=1,
            grid=(1,),
            in_specs=[whole(lookups, samples)] * 4
            + [whole(samples, width)] * 2
            + [whole(blocks, block, width)],
            out_specs=[whole(block, width)] * depth + [whole(samples, width)] * 2,
            scratch_shapes=[
                pltpu.VMEM((block, 2 * samples), jnp.bfloat16),
                pltpu.VMEM((width, 2 * samples), jnp.float32),
                pltpu.VMEM((depth, block, width), jnp.float32),
            ],
        ),
        out_shape=[jax.ShapeDtypeStruct((block, width), jnp.float32)] * depth
        + [jax.ShapeDtypeStruct((samples, width), jnp.float32)] * 2,
        compiler_params=pltpu.CompilerParams(vmem_limit_bytes=60 << 20),
        cost_estimate=pl.CostEstimate(
            flops=8 * samples * depth * block * width,
            bytes_accessed=2 * samples * depth * block * 16,
            transcendentals=0,
        ),
        name="hot",
    )(place, *pairs, table)


def shift(axis, size, by, value):
    return lax.ppermute(value, axis, [(i, (i + by) % size) for i in range(size)])


def shards(
    cold_table, slot_row, slot_sample, slot_count, hot_table, hot_index, hot_count, hot_cotangent
):
    samples = hot_index.shape[0]
    width = cold_table.shape[1]
    side = lax.axis_size("x")
    depth = lax.axis_size("z")
    y, x, z, core = (lax.axis_index(axis) for axis in ALL)
    place = jnp.stack([z, core, y, x])

    asked = pack([slot_row, slot_sample, slot_count])
    requests = lax.all_to_all(asked, ("y", "x"), split_axis=0, concat_axis=0, tiled=True)

    pairs = []
    for value in (hot_index.T, hot_count.T, hot_cotangent):
        pairs += [value, shift("core", 2, 1, value)]
    blocks = hot_table.reshape(2 * depth, -1, width)
    *grads, hot_own, hot_other = hot_call(place, pairs, blocks, depth)
    hot_got = shift("core", 2, 1, hot_other)
    parts = [grads[0]] + [shift("z", depth, by, grads[by]) for by in range(1, depth)]

    cold_table, requests, hot_got, place = lax.optimization_barrier(
        (cold_table, requests, hot_got, place)
    )
    wide = widen(cold_table)
    sent = pool_far(place, requests, wide, samples)
    *sent, share = attach(parts, sent)
    got = [shift("x", side, i + 1, sent[i]) for i in range(3)] + [
        shift("y", side, i + 1, sent[3 + i]) for i in range(3)
    ]
    close = pool_near("pool_near", near_source, 6, place, requests, wide, samples)
    passed = relay(close, share, got)
    last = [shift("y", side, i + 1, passed[i]) for i in range(3)] + [
        shift("x", side, i + 1, passed[3 + i]) for i in range(3)
    ]
    home = pool_near("pool_own", own_source, 1, place, requests, wide, samples)
    features, hot_grad = finish(home, passed[0], passed[3], last, hot_own, hot_got)
    return (features, hot_grad)


def solution(mesh):
    fine = Mesh(mesh.devices.reshape(4, 4, 8, 2), ALL)
    every = P(ALL, None)
    return jax.shard_map(
        shards,
        mesh=fine,
        in_specs=(P(("y", "x"), None), every, every, every, P(), every, every, every),
        out_specs=(every, P(("z", "core"), None)),
        check_vma=False,
    )
```

```python
import functools

import jax
import jax.numpy as jnp
from jax import lax
from jax.experimental import pallas as pl
from jax.experimental.pallas import tpu as pltpu
from jax.sharding import Mesh, PartitionSpec as P

cold_scale = 0.03125
hot_scale = 0.0625
CHUNK = 128
PAD = 8
ALL = ("y", "x", "z", "core")


def widen_kernel(table_hbm, wide_ref, buf, sem):
    steps = sem.shape[0]
    rows = buf.shape[0] // steps

    def fetch(step):
        part = pl.ds(step * rows, rows)
        return pltpu.make_async_copy(table_hbm.at[part], buf.at[part], sem.at[step])

    for step in range(steps):
        fetch(step).start()
    edge = jnp.zeros((PAD, wide_ref.shape[1]), jnp.float32)
    wide_ref[:PAD] = edge
    wide_ref[wide_ref.shape[0] - PAD :] = edge
    for step in range(steps):
        fetch(step).wait()
        part = slice(step * rows, (step + 1) * rows)
        wide_ref[PAD + step * rows : PAD + (step + 1) * rows] = buf[part].astype(jnp.float32)


def widen(table):
    rows, width = table.shape
    return pl.pallas_call(
        widen_kernel,
        in_specs=[pl.BlockSpec(memory_space=pl.ANY)],
        out_specs=pl.BlockSpec(memory_space=pltpu.VMEM),
        out_shape=pltpu.VMEM((rows + 2 * PAD, width), jnp.float32),
        scratch_shapes=[
            pltpu.VMEM((rows, width), jnp.bfloat16),
            pltpu.SemaphoreType.DMA((16,)),
        ],
        compiler_params=pltpu.CompilerParams(vmem_limit_bytes=44 << 20),
        cost_estimate=pl.CostEstimate(
            flops=rows * width, bytes_accessed=rows * width * 6, transcendentals=0
        ),
        name="widen",
    )(table)


def pack_kernel(a, b, c, out):
    for part, ref in enumerate((a, b, c)):
        for bucket in range(ref.shape[0]):
            out[bucket, part : part + 1, :] = ref[bucket : bucket + 1, :]


def pack(parts):
    buckets, slots = parts[0].shape
    return pl.pallas_call(
        pack_kernel,
        grid=(1,),
        in_specs=[pl.BlockSpec((buckets, slots), lambda i: (0, 0))] * 3,
        out_specs=pl.BlockSpec((buckets, 3, slots), lambda i: (0, 0, 0)),
        out_shape=jax.ShapeDtypeStruct((buckets, 3, slots), jnp.int32),
        compiler_params=pltpu.CompilerParams(vmem_limit_bytes=60 << 20),
        cost_estimate=pl.CostEstimate(
            flops=0, bytes_accessed=buckets * slots * 24, transcendentals=0
        ),
        name="pack",
    )(*parts)


def pool_task(rows_ref, slots_ref, wide_ref, acc, bufs):
    slots = rows_ref.shape[2]
    samples, width = acc.shape
    sublane = lax.broadcasted_iota(jnp.int32, (PAD, width), 0)

    def gather(chunk):
        buf = bufs[chunk % 2]
        for tile in range(CHUNK // PAD):
            merged = None
            for lane in range(PAD):
                row = rows_ref[0, 0, chunk * CHUNK + tile * PAD + lane]
                near = wide_ref[pl.ds(row + (PAD - lane), PAD), :]
                merged = near if lane == 0 else jnp.where(sublane == lane, near, merged)
            buf[tile * PAD : (tile + 1) * PAD, :] = merged

    def pool(chunk):
        cols = slice(chunk * CHUNK, (chunk + 1) * CHUNK)
        ids = lax.broadcasted_iota(jnp.int32, (samples, CHUNK), 0)
        weight = slots_ref[0, 2:3, cols].astype(jnp.float32) * cold_scale
        weights = jnp.where(ids == slots_ref[0, 1:2, cols], weight, 0.0).astype(jnp.bfloat16)
        part = jnp.dot(
            weights,
            bufs[chunk % 2][...].astype(jnp.bfloat16),
            preferred_element_type=jnp.float32,
        )
        if chunk == 0:
            acc[...] = part
        else:
            acc[...] += part

    gather(0)
    for chunk in range(slots // CHUNK):
        if (chunk + 1) * CHUNK < slots:
            gather(chunk + 1)
        pool(chunk)


def far_kernel(place, rows_ref, slots_ref, wide_ref, *refs):
    del place
    outs, (acc, buf0, buf1) = refs[:6], refs[6:]
    pool_task(rows_ref, slots_ref, wide_ref, acc, (buf0, buf1))
    task = pl.program_id(0)
    half = acc.shape[0] // 2
    part = half // 2
    for i in range(3):

        @pl.when(task // 3 == i)
        def _():
            outs[i][0] = acc[:part]
            outs[i][1] = acc[part:half]

        @pl.when(task % 3 == i)
        def _():
            outs[3 + i][0] = acc[half : half + part]
            outs[3 + i][1] = acc[half + part :]


def near_kernel(place, rows_ref, slots_ref, wide_ref, out, acc, buf0, buf1):
    del place
    pool_task(rows_ref, slots_ref, wide_ref, acc, (buf0, buf1))
    out[0] = acc[...]


def source(place, dy, dx):
    return ((place[2] + dy) & 3) * 4 + ((place[3] + dx) & 3)


def far_source(t, place):
    return source(place, t % 3 + 1, t // 3 + 1)


def near_source(t, place):
    return source(place, jnp.where(t < 3, t + 1, 0), jnp.where(t < 3, 0, t - 2))


def own_source(t, place):
    return source(place, 0, 0)


def pool_call(body, name, origin, tasks, place, requests, wide, samples, out_specs, out_shape):
    _, parts, slots = requests.shape
    width = wide.shape[1]

    def spec(space):
        return pl.BlockSpec(
            (1, parts, slots), lambda t, place: (origin(t, place), 0, 0), memory_space=space
        )

    return pl.pallas_call(
        body,
        grid_spec=pltpu.PrefetchScalarGridSpec(
            num_scalar_prefetch=1,
            grid=(tasks,),
            in_specs=[spec(pltpu.SMEM), spec(pltpu.VMEM), pl.BlockSpec(memory_space=pltpu.VMEM)],
            out_specs=out_specs,
            scratch_shapes=[pltpu.VMEM((samples, width), jnp.float32)]
            + [pltpu.VMEM((CHUNK, width), jnp.float32)] * 2,
        ),
        out_shape=out_shape,
        compiler_params=pltpu.CompilerParams(vmem_limit_bytes=20 << 20),
        cost_estimate=pl.CostEstimate(
            flops=tasks * 2 * samples * slots * width,
            bytes_accessed=tasks * slots * width * 20,
            transcendentals=0,
        ),
        name=name,
    )(place, requests, requests, wide)


def pool_far(place, requests, wide, samples):
    width = wide.shape[1]
    part = samples // 4
    specs = [
        pl.BlockSpec(
            (2, part, width), lambda t, place, i=i: (jnp.clip(t - 3 * i, 0, 2), 0, 0)
        )
        for i in range(3)
    ] + [
        pl.BlockSpec(
            (2, part, width),
            lambda t, place, i=i: (jnp.clip((t - i + 3) // 3 - 1, 0, 2), 0, 0),
        )
        for i in range(3)
    ]
    shape = [jax.ShapeDtypeStruct((7, part, width), jnp.float32)] * 6
    return pool_call(
        far_kernel, "pool_far", far_source, 9, place, requests, wide, samples, specs, shape
    )


def pool_near(name, origin, tasks, place, requests, wide, samples):
    width = wide.shape[1]
    return pool_call(
        near_kernel,
        name,
        origin,
        tasks,
        place,
        requests,
        wide,
        samples,
        pl.BlockSpec((1, samples, width), lambda t, place: (t, 0, 0)),
        jax.ShapeDtypeStruct((tasks, samples, width), jnp.float32),
    )


def attach_kernel(*refs):
    parts, outs, share_ref = refs[:8], refs[14:20], refs[20]
    p = [ref[...] for ref in parts]
    share = ((p[0] + p[1]) + (p[2] + p[3])) + ((p[4] + p[5]) + (p[6] + p[7]))
    share_ref[...] = share
    half = share.shape[0] // 2
    for out in outs[:3]:
        out[0] = share[:half]
    for out in outs[3:]:
        out[0] = share[half:]


def attach(parts, sent):
    block, width = parts[0].shape
    last = pl.BlockSpec((1, block // 2, width), lambda i: (6, 0, 0))
    whole = pl.BlockSpec((block, width), lambda i: (0, 0))
    return pl.pallas_call(
        attach_kernel,
        grid=(1,),
        in_specs=[whole] * 8 + [pl.BlockSpec(memory_space=pl.ANY)] * 6,
        out_specs=[last] * 6 + [whole],
        out_shape=[jax.ShapeDtypeStruct(sent[0].shape, jnp.float32)] * 6
        + [jax.ShapeDtypeStruct((block, width), jnp.float32)],
        input_output_aliases={8 + i: i for i in range(6)},
        compiler_params=pltpu.CompilerParams(vmem_limit_bytes=8 << 20),
        cost_estimate=pl.CostEstimate(
            flops=block * width * 8, bytes_accessed=block * width * 48, transcendentals=0
        ),
        name="attach",
    )(*parts, *sent)


def relay_kernel(near_ref, share_ref, *refs):
    got, outs = refs[:6], refs[6:]
    samples = near_ref.shape[1]
    half = samples // 2
    part = half // 2
    for s, (way, rows) in enumerate(((got[:3], slice(0, part)), (got[3:], slice(part, half)))):
        one, two, three = way
        share = (share_ref[rows] + two[6]) + (one[6] + three[6])
        for i in range(3):
            near, out = near_ref.at[3 * s + i], outs[3 * s + i]
            direct = slice(half, samples) if s == 0 else slice(0, half)
            out[direct] = near[direct]
            out[samples:] = share
            for q in range(2):
                at = slice(s * half + q * part, s * half + (q + 1) * part)
                out[at] = near[at] + (one[2 * i + q] + two[2 * i + q] + three[2 * i + q])


def relay(near, share, got):
    _, samples, width = near.shape
    tall = samples + share.shape[0] // 2
    return pl.pallas_call(
        relay_kernel,
        out_shape=[jax.ShapeDtypeStruct((tall, width), jnp.float32)] * 6,
        compiler_params=pltpu.CompilerParams(vmem_limit_bytes=16 << 20),
        cost_estimate=pl.CostEstimate(
            flops=samples * width * 12, bytes_accessed=samples * width * 84, transcendentals=0
        ),
        name="relay",
    )(near, share, *got)


def finish_kernel(near_ref, mine0, mine1, a, b, c, d, e, f, hot_own, hot_got, out, grad):
    samples, width = hot_own.shape
    half = grad.shape[0] // 2
    cold = near_ref[0] + (
        (a[:samples] + b[:samples] + c[:samples]) + (d[:samples] + e[:samples] + f[:samples])
    )
    out[:, :width] = cold.astype(jnp.bfloat16)
    out[:, width:] = (hot_own[...] + hot_got[...]).astype(jnp.bfloat16)
    grad[:half] = (mine0[samples:] + b[samples:]) + (a[samples:] + c[samples:])
    grad[half:] = (mine1[samples:] + e[samples:]) + (d[samples:] + f[samples:])


def finish(near, mine0, mine1, got, hot_own, hot_got):
    _, samples, width = near.shape
    tall = mine0.shape[0]
    whole = pl.BlockSpec((samples, width), lambda i: (0, 0))
    more = pl.BlockSpec((tall, width), lambda i: (0, 0))
    share = 2 * (tall - samples)
    return pl.pallas_call(
        finish_kernel,
        grid=(1,),
        in_specs=[pl.BlockSpec((1, samples, width), lambda i: (0, 0, 0))]
        + [more] * 8
        + [whole] * 2,
        out_specs=[
            pl.BlockSpec((samples, 2 * width), lambda i: (0, 0)),
            pl.BlockSpec((share, width), lambda i: (0, 0)),
        ],
        out_shape=[
            jax.ShapeDtypeStruct((samples, 2 * width), jnp.bfloat16),
            jax.ShapeDtypeStruct((share, width), jnp.float32),
        ],
        compiler_params=pltpu.CompilerParams(vmem_limit_bytes=16 << 20),
        cost_estimate=pl.CostEstimate(
            flops=samples * width * 8, bytes_accessed=samples * width * 40, transcendentals=0
        ),
        name="finish",
    )(near, mine0, mine1, *got, hot_own, hot_got)


def hot_kernel(place, idx0, idx1, cnt0, cnt1, cot0, cot1, table_ref, *refs):
    grads, (own_ref, other_ref, inc, pooled, held) = refs[:8], refs[8:]
    block = table_ref.shape[1]
    lookups, samples = idx0.shape
    depth = held.shape[0]
    lanes = 128
    tile = 16

    def step(ahead, carry):
        blk = 2 * lax.rem(place[0] + ahead, depth) + place[1]
        start = blk * block
        for lane in range(2 * samples // lanes):
            idx_ref, cnt_ref = (idx0, cnt0) if lane * lanes < samples else (idx1, cnt1)
            first = lane * lanes % samples
            cols = slice(first, first + lanes)
            to = slice(lane * lanes, (lane + 1) * lanes)
            local = jnp.clip(idx_ref[:, cols] - start, -1, block)
            weight = cnt_ref[:, cols].astype(jnp.float32) * hot_scale
            keys = []
            for k in range(lookups):
                keys.append(
                    (
                        jnp.broadcast_to(local[k : k + 1], (tile, lanes)).astype(jnp.int16),
                        jnp.broadcast_to(weight[k : k + 1], (tile, lanes)).astype(jnp.bfloat16),
                    )
                )
            base = lax.broadcasted_iota(jnp.int32, (tile, lanes), 0)
            for group in range(block // tile):
                ids = (base + group * tile).astype(jnp.int16)
                total = jnp.zeros((tile, lanes), jnp.bfloat16)
                for key, value in keys:
                    total = total + jnp.where(ids == key, value, jnp.bfloat16(0))
                inc[group * tile : (group + 1) * tile, to] = total
        held[ahead] = jnp.dot(
            inc[:, :samples], cot0[...], preferred_element_type=jnp.float32
        ) + jnp.dot(inc[:, samples:], cot1[...], preferred_element_type=jnp.float32)
        part = lax.dot_general(
            table_ref[blk],
            inc[...],
            (((0,), (0,)), ((), ())),
            preferred_element_type=jnp.float32,
        )

        @pl.when(ahead == 0)
        def _():
            pooled[...] = part

        @pl.when(ahead > 0)
        def _():
            pooled[...] += part

        return carry

    lax.fori_loop(0, depth, step, 0)
    own_ref[...] = jnp.transpose(pooled[:, :samples])
    other_ref[...] = jnp.transpose(pooled[:, samples:])
    for ahead in range(depth):
        grads[ahead][...] = held[ahead]


def hot_call(place, pairs, table, depth):
    blocks, block, width = table.shape
    lookups, samples = pairs[0].shape

    def whole(*shape):
        return pl.BlockSpec(shape, lambda i, place: (0,) * len(shape))

    return pl.pallas_call(
        hot_kernel,
        grid_spec=pltpu.PrefetchScalarGridSpec(
            num_scalar_prefetch=1,
            grid=(1,),
            in_specs=[whole(lookups, samples)] * 4
            + [whole(samples, width)] * 2
            + [whole(blocks, block, width)],
            out_specs=[whole(block, width)] * depth + [whole(samples, width)] * 2,
            scratch_shapes=[
                pltpu.VMEM((block, 2 * samples), jnp.bfloat16),
                pltpu.VMEM((width, 2 * samples), jnp.float32),
                pltpu.VMEM((depth, block, width), jnp.float32),
            ],
        ),
        out_shape=[jax.ShapeDtypeStruct((block, width), jnp.float32)] * depth
        + [jax.ShapeDtypeStruct((samples, width), jnp.float32)] * 2,
        compiler_params=pltpu.CompilerParams(vmem_limit_bytes=60 << 20),
        cost_estimate=pl.CostEstimate(
            flops=8 * samples * depth * block * width,
            bytes_accessed=2 * samples * depth * block * 16,
            transcendentals=0,
        ),
        name="hot",
    )(place, *pairs, table)


def shift(axis, size, by, value):
    return lax.ppermute(value, axis, [(i, (i + by) % size) for i in range(size)])


def shards(
    cold_table, slot_row, slot_sample, slot_count, hot_table, hot_index, hot_count, hot_cotangent
):
    samples = hot_index.shape[0]
    width = cold_table.shape[1]
    side = lax.axis_size("x")
    depth = lax.axis_size("z")
    y, x, z, core = (lax.axis_index(axis) for axis in ALL)
    place = jnp.stack([z, core, y, x])

    asked = pack([slot_row, slot_sample, slot_count])
    requests = lax.all_to_all(asked, ("y", "x"), split_axis=0, concat_axis=0, tiled=True)

    pairs = []
    for value in (hot_index.T, hot_count.T, hot_cotangent):
        pairs += [value, shift("core", 2, 1, value)]
    blocks = hot_table.reshape(2 * depth, -1, width)
    *grads, hot_own, hot_other = hot_call(place, pairs, blocks, depth)
    hot_got = shift("core", 2, 1, hot_other)
    parts = [grads[0]] + [shift("z", depth, by, grads[by]) for by in range(1, depth)]

    cold_table, requests, hot_got, place = lax.optimization_barrier(
        (cold_table, requests, hot_got, place)
    )
    wide = widen(cold_table)
    sent = pool_far(place, requests, wide, samples)
    *sent, share = attach(parts, sent)
    got = [shift("x", side, i + 1, sent[i]) for i in range(3)] + [
        shift("y", side, i + 1, sent[3 + i]) for i in range(3)
    ]
    close = pool_near("pool_near", near_source, 6, place, requests, wide, samples)
    passed = relay(close, share, got)
    last = [shift("y", side, i + 1, passed[i]) for i in range(3)] + [
        shift("x", side, i + 1, passed[3 + i]) for i in range(3)
    ]
    home = pool_near("pool_own", own_source, 1, place, requests, wide, samples)
    features, hot_grad = finish(home, passed[0], passed[3], last, hot_own, hot_got)
    return (features, hot_grad)


def solution(mesh):
    fine = Mesh(mesh.devices.reshape(4, 4, 8, 2), ALL)
    every = P(ALL, None)
    return jax.shard_map(
        shards,
        mesh=fine,
        in_specs=(P(("y", "x"), None), every, every, every, P(), every, every, every),
        out_specs=(every, P(("z", "core"), None)),
        check_vma=False,
    )
```

```python
import jax
import jax.numpy as jnp
from jax import lax
from jax.experimental import pallas as pl
from jax.experimental.pallas import tpu as pltpu
from jax.sharding import Mesh, PartitionSpec as P


cold_scale = 0.03125
hot_scale = 0.0625
CHUNK = 128
PAD = 8
ALL = ("y", "x", "z", "core")


def widen_kernel(table_hbm, wide_ref, buf, sem):
    steps = sem.shape[0]
    rows = buf.shape[0] // steps

    def fetch(step):
        part = pl.ds(step * rows, rows)
        return pltpu.make_async_copy(table_hbm.at[part], buf.at[part], sem.at[step])

    for step in range(steps):
        fetch(step).start()
    edge = jnp.zeros((PAD, wide_ref.shape[1]), jnp.float32)
    wide_ref[:PAD] = edge
    wide_ref[wide_ref.shape[0] - PAD :] = edge
    for step in range(steps):
        fetch(step).wait()
        part = slice(step * rows, (step + 1) * rows)
        wide_ref[PAD + step * rows : PAD + (step + 1) * rows] = buf[part].astype(jnp.float32)


def widen(table):
    rows, width = table.shape
    return pl.pallas_call(
        widen_kernel,
        in_specs=[pl.BlockSpec(memory_space=pl.ANY)],
        out_specs=pl.BlockSpec(memory_space=pltpu.VMEM),
        out_shape=pltpu.VMEM((rows + 2 * PAD, width), jnp.float32),
        scratch_shapes=[
            pltpu.VMEM((rows, width), jnp.bfloat16),
            pltpu.SemaphoreType.DMA((16,)),
        ],
        compiler_params=pltpu.CompilerParams(vmem_limit_bytes=44 << 20),
        cost_estimate=pl.CostEstimate(
            flops=rows * width, bytes_accessed=rows * width * 6, transcendentals=0
        ),
        name="widen",
    )(table)


def pack_kernel(a, b, c, out):
    for part, ref in enumerate((a, b, c)):
        for bucket in range(ref.shape[0]):
            out[bucket, part : part + 1, :] = ref[bucket : bucket + 1, :]


def pack(parts):
    buckets, slots = parts[0].shape
    return pl.pallas_call(
        pack_kernel,
        grid=(1,),
        in_specs=[pl.BlockSpec((buckets, slots), lambda i: (0, 0))] * 3,
        out_specs=pl.BlockSpec((buckets, 3, slots), lambda i: (0, 0, 0)),
        out_shape=jax.ShapeDtypeStruct((buckets, 3, slots), jnp.int32),
        compiler_params=pltpu.CompilerParams(vmem_limit_bytes=60 << 20),
        cost_estimate=pl.CostEstimate(
            flops=0, bytes_accessed=buckets * slots * 24, transcendentals=0
        ),
        name="pack",
    )(*parts)


def pool_task(rows_ref, slots_ref, wide_ref, acc, bufs):
    slots = rows_ref.shape[2]
    samples, width = acc.shape
    sublane = lax.broadcasted_iota(jnp.int32, (PAD, width), 0)

    def gather(chunk):
        buf = bufs[chunk % 2]
        for tile in range(CHUNK // PAD):
            merged = None
            for lane in range(PAD):
                row = rows_ref[0, 0, chunk * CHUNK + tile * PAD + lane]
                near = wide_ref[pl.ds(row + (PAD - lane), PAD), :]
                merged = near if lane == 0 else jnp.where(sublane == lane, near, merged)
            buf[tile * PAD : (tile + 1) * PAD, :] = merged

    def pool(chunk):
        cols = slice(chunk * CHUNK, (chunk + 1) * CHUNK)
        ids = lax.broadcasted_iota(jnp.int32, (samples, CHUNK), 0)
        weight = slots_ref[0, 2:3, cols].astype(jnp.float32) * cold_scale
        weights = jnp.where(ids == slots_ref[0, 1:2, cols], weight, 0.0).astype(jnp.bfloat16)
        part = jnp.dot(
            weights,
            bufs[chunk % 2][...].astype(jnp.bfloat16),
            preferred_element_type=jnp.float32,
        )
        if chunk == 0:
            acc[...] = part
        else:
            acc[...] += part

    gather(0)
    for chunk in range(slots // CHUNK):
        if (chunk + 1) * CHUNK < slots:
            gather(chunk + 1)
        pool(chunk)


def far_kernel(place, rows_ref, slots_ref, wide_ref, *refs):
    del place
    (out_x, *outs_y), (acc, buf0, buf1) = refs[-7:-3], refs[-3:]
    pool_task(rows_ref, slots_ref, wide_ref, acc, (buf0, buf1))
    task = pl.program_id(0)
    half = acc.shape[0] // 2
    part = half // 2
    out_x[0] = acc[:part]
    out_x[1] = acc[part:half]
    for i in range(3):

        @pl.when(task == i)
        def _():
            outs_y[i][0] = acc[half : half + part]
            outs_y[i][1] = acc[half + part :]


def near_kernel(place, rows_ref, slots_ref, wide_ref, out, acc, buf0, buf1):
    del place
    pool_task(rows_ref, slots_ref, wide_ref, acc, (buf0, buf1))
    out[0] = acc[...]


def source(place, dy, dx):
    return ((place[2] + dy) & 3) * 4 + ((place[3] + dx) & 3)


def near_source(t, place):
    return source(place, jnp.where(t < 3, t + 1, 0), jnp.where(t < 3, 0, t - 2))


def own_source(t, place):
    return source(place, 0, 0)


def pool_call(body, origin, tasks, place, requests, wide, samples, out_specs, out_shape, held=()):
    _, parts, slots = requests.shape
    width = wide.shape[1]

    def spec(space):
        return pl.BlockSpec(
            (1, parts, slots), lambda t, place: (origin(t, place), 0, 0), memory_space=space
        )

    return pl.pallas_call(
        body,
        grid_spec=pltpu.PrefetchScalarGridSpec(
            num_scalar_prefetch=1,
            grid=(tasks,),
            in_specs=[spec(pltpu.SMEM), spec(pltpu.VMEM), pl.BlockSpec(memory_space=pltpu.VMEM)]
            + [pl.BlockSpec(memory_space=pl.ANY)] * len(held),
            out_specs=out_specs,
            scratch_shapes=[pltpu.VMEM((samples, width), jnp.float32)]
            + [pltpu.VMEM((CHUNK, width), jnp.float32)] * 2,
        ),
        out_shape=out_shape,
        input_output_aliases={4 + i: 1 + i for i in range(len(held))},
        compiler_params=pltpu.CompilerParams(vmem_limit_bytes=20 << 20),
        cost_estimate=pl.CostEstimate(
            flops=tasks * 2 * samples * slots * width,
            bytes_accessed=tasks * slots * width * 20,
            transcendentals=0,
        ),
    )(place, requests, requests, wide, *held)


def pool_far(dx, place, requests, wide, samples, held):
    width = wide.shape[1]
    part = samples // 4

    def origin(t, place):
        return source(place, t + 1, dx)

    specs = [pl.BlockSpec((2, part, width), lambda t, place: (t, 0, 0))] + [
        pl.BlockSpec((2, part, width), lambda t, place: (dx - 1, 0, 0))
    ] * 3
    shape = [jax.ShapeDtypeStruct((6, part, width), jnp.float32)] + [
        jax.ShapeDtypeStruct((8, part, width), jnp.float32)
    ] * 3
    return pool_call(far_kernel, origin, 3, place, requests, wide, samples, specs, shape, held)


def pool_near(origin, tasks, place, requests, wide, samples):
    width = wide.shape[1]
    return pool_call(
        near_kernel,
        origin,
        tasks,
        place,
        requests,
        wide,
        samples,
        pl.BlockSpec((1, samples, width), lambda t, place: (t, 0, 0)),
        jax.ShapeDtypeStruct((tasks, samples, width), jnp.float32),
    )


def attach_kernel(*refs):
    parts, outs, share_ref = refs[:8], refs[11:14], refs[14]
    p = [ref[...] for ref in parts]
    share = ((p[0] + p[1]) + (p[2] + p[3])) + ((p[4] + p[5]) + (p[6] + p[7]))
    share_ref[...] = share
    half = share.shape[0] // 2
    for out in outs:
        out[0] = share[:half]
        out[1] = share[half:]


def attach(parts, sent):
    block, width = parts[0].shape
    last = pl.BlockSpec((2, block // 2, width), lambda i: (3, 0, 0))
    whole = pl.BlockSpec((block, width), lambda i: (0, 0))
    return pl.pallas_call(
        attach_kernel,
        grid=(1,),
        in_specs=[whole] * 8 + [pl.BlockSpec(memory_space=pl.ANY)] * 3,
        out_specs=[last] * 3 + [whole],
        out_shape=[jax.ShapeDtypeStruct(sent[0].shape, jnp.float32)] * 3
        + [jax.ShapeDtypeStruct((block, width), jnp.float32)],
        input_output_aliases={8 + i: i for i in range(3)},
        compiler_params=pltpu.CompilerParams(vmem_limit_bytes=8 << 20),
        cost_estimate=pl.CostEstimate(
            flops=block * width * 8, bytes_accessed=block * width * 48, transcendentals=0
        ),
        name="attach",
    )(*parts, *sent)


def relay_kernel(near_ref, share_ref, *refs):
    got, outs = refs[:6], refs[6:]
    samples = near_ref.shape[1]
    half = samples // 2
    part = half // 2
    for q in range(2):
        rows = slice(q * part, (q + 1) * part)
        to = slice(samples + q * part, samples + (q + 1) * part)
        share = (share_ref[rows] + got[4][6 + q]) + (got[3][6 + q] + got[5][6 + q])
        for i in range(3):
            outs[3 + i][to] = share
    for s, (one, two, three) in enumerate((got[:3], got[3:])):
        for i in range(3):
            near, out = near_ref.at[3 * s + i], outs[3 * s + i]
            direct = slice(half, samples) if s == 0 else slice(0, half)
            out[direct] = near[direct]
            for q in range(2):
                at = slice(s * half + q * part, s * half + (q + 1) * part)
                out[at] = near[at] + (one[2 * i + q] + two[2 * i + q] + three[2 * i + q])


def relay(near, share, got):
    _, samples, width = near.shape
    tall = samples + share.shape[0]
    return pl.pallas_call(
        relay_kernel,
        out_shape=[jax.ShapeDtypeStruct((samples, width), jnp.float32)] * 3
        + [jax.ShapeDtypeStruct((tall, width), jnp.float32)] * 3,
        compiler_params=pltpu.CompilerParams(vmem_limit_bytes=16 << 20),
        cost_estimate=pl.CostEstimate(
            flops=samples * width * 12, bytes_accessed=samples * width * 84, transcendentals=0
        ),
        name="relay",
    )(near, share, *got)


def finish_kernel(near_ref, mine, a, b, c, d, e, f, hot_own, hot_got, out, grad):
    samples, width = hot_own.shape
    cold = near_ref[0] + (
        (a[...] + b[...] + c[...]) + (d[:samples] + e[:samples] + f[:samples])
    )
    out[:, :width] = cold.astype(jnp.bfloat16)
    out[:, width:] = (hot_own[...] + hot_got[...]).astype(jnp.bfloat16)
    grad[...] = (mine[samples:] + e[samples:]) + (d[samples:] + f[samples:])


def finish(near, mine, got, hot_own, hot_got):
    _, samples, width = near.shape
    tall = mine.shape[0]
    whole = pl.BlockSpec((samples, width), lambda i: (0, 0))
    more = pl.BlockSpec((tall, width), lambda i: (0, 0))
    return pl.pallas_call(
        finish_kernel,
        grid=(1,),
        in_specs=[pl.BlockSpec((1, samples, width), lambda i: (0, 0, 0)), more]
        + [whole] * 3
        + [more] * 3
        + [whole] * 2,
        out_specs=[
            pl.BlockSpec((samples, 2 * width), lambda i: (0, 0)),
            pl.BlockSpec((tall - samples, width), lambda i: (0, 0)),
        ],
        out_shape=[
            jax.ShapeDtypeStruct((samples, 2 * width), jnp.bfloat16),
            jax.ShapeDtypeStruct((tall - samples, width), jnp.float32),
        ],
        compiler_params=pltpu.CompilerParams(vmem_limit_bytes=16 << 20),
        cost_estimate=pl.CostEstimate(
            flops=samples * width * 8, bytes_accessed=samples * width * 40, transcendentals=0
        ),
        name="finish",
    )(near, mine, *got, hot_own, hot_got)


def hot_kernel(place, idx0, idx1, cnt0, cnt1, cot0, cot1, table_ref, *refs):
    grads, (own_ref, other_ref, inc, pooled, held) = refs[:8], refs[8:]
    block = table_ref.shape[1]
    lookups, samples = idx0.shape
    depth = held.shape[0]
    lanes = 128
    tile = 16

    def step(ahead, carry):
        blk = 2 * lax.rem(place[0] + ahead, depth) + place[1]
        start = blk * block
        for lane in range(2 * samples // lanes):
            idx_ref, cnt_ref = (idx0, cnt0) if lane * lanes < samples else (idx1, cnt1)
            first = lane * lanes % samples
            cols = slice(first, first + lanes)
            to = slice(lane * lanes, (lane + 1) * lanes)
            local = jnp.clip(idx_ref[:, cols] - start, -1, block)
            weight = cnt_ref[:, cols].astype(jnp.float32) * hot_scale
            keys = []
            for k in range(lookups):
                keys.append(
                    (
                        jnp.broadcast_to(local[k : k + 1], (tile, lanes)).astype(jnp.int16),
                        jnp.broadcast_to(weight[k : k + 1], (tile, lanes)).astype(jnp.bfloat16),
                    )
                )
            base = lax.broadcasted_iota(jnp.int32, (tile, lanes), 0)
            for group in range(block // tile):
                ids = (base + group * tile).astype(jnp.int16)
                total = jnp.zeros((tile, lanes), jnp.bfloat16)
                for key, value in keys:
                    total = total + jnp.where(ids == key, value, jnp.bfloat16(0))
                inc[group * tile : (group + 1) * tile, to] = total
        held[ahead] = jnp.dot(
            inc[:, :samples], cot0[...], preferred_element_type=jnp.float32
        ) + jnp.dot(inc[:, samples:], cot1[...], preferred_element_type=jnp.float32)
        part = lax.dot_general(
            table_ref[blk],
            inc[...],
            (((0,), (0,)), ((), ())),
            preferred_element_type=jnp.float32,
        )

        @pl.when(ahead == 0)
        def _():
            pooled[...] = part

        @pl.when(ahead > 0)
        def _():
            pooled[...] += part

        return carry

    lax.fori_loop(0, depth, step, 0)
    own_ref[...] = jnp.transpose(pooled[:, :samples])
    other_ref[...] = jnp.transpose(pooled[:, samples:])
    for ahead in range(depth):
        grads[ahead][...] = held[ahead]


def hot_call(place, pairs, table, depth):
    blocks, block, width = table.shape
    lookups, samples = pairs[0].shape

    def whole(*shape):
        return pl.BlockSpec(shape, lambda i, place: (0,) * len(shape))

    return pl.pallas_call(
        hot_kernel,
        grid_spec=pltpu.PrefetchScalarGridSpec(
            num_scalar_prefetch=1,
            grid=(1,),
            in_specs=[whole(lookups, samples)] * 4
            + [whole(samples, width)] * 2
            + [whole(blocks, block, width)],
            out_specs=[whole(block, width)] * depth + [whole(samples, width)] * 2,
            scratch_shapes=[
                pltpu.VMEM((block, 2 * samples), jnp.bfloat16),
                pltpu.VMEM((width, 2 * samples), jnp.float32),
                pltpu.VMEM((depth, block, width), jnp.float32),
            ],
        ),
        out_shape=[jax.ShapeDtypeStruct((block, width), jnp.float32)] * depth
        + [jax.ShapeDtypeStruct((samples, width), jnp.float32)] * 2,
        compiler_params=pltpu.CompilerParams(vmem_limit_bytes=60 << 20),
        cost_estimate=pl.CostEstimate(
            flops=8 * samples * depth * block * width,
            bytes_accessed=2 * samples * depth * block * 16,
            transcendentals=0,
        ),
        name="hot",
    )(place, *pairs, table)


def shift(axis, size, by, value):
    return lax.ppermute(value, axis, [(i, (i + by) % size) for i in range(size)])


def shards(
    cold_table, slot_row, slot_sample, slot_count, hot_table, hot_index, hot_count, hot_cotangent
):
    samples = hot_index.shape[0]
    width = cold_table.shape[1]
    side = lax.axis_size("x")
    depth = lax.axis_size("z")
    y, x, z, core = (lax.axis_index(axis) for axis in ALL)
    place = jnp.stack([z, core, y, x])

    asked = pack([slot_row, slot_sample, slot_count])
    requests = lax.all_to_all(asked, ("y", "x"), split_axis=0, concat_axis=0, tiled=True)

    pairs = []
    for value in (hot_index.T, hot_count.T, hot_cotangent):
        pairs += [value, shift("core", 2, 1, value)]
    blocks = hot_table.reshape(2 * depth, -1, width)
    *grads, hot_own, hot_other = hot_call(place, pairs, blocks, depth)
    hot_got = shift("core", 2, 1, hot_other)
    parts = [grads[0]] + [shift("z", depth, by, grads[by]) for by in range(1, depth)]

    cold_table, requests, hot_got, place = lax.optimization_barrier(
        (cold_table, requests, hot_got, place)
    )
    wide = widen(cold_table)
    got_x, held = [], ()
    for dx in (1, 2, 3):
        out_x, *held = pool_far(dx, place, requests, wide, samples, held)
        got_x.append(shift("x", side, dx, out_x))
    *held, share = attach(parts, held)
    got = got_x + [shift("y", side, i + 1, held[i]) for i in range(3)]
    close = pool_near(near_source, 6, place, requests, wide, samples)
    passed = relay(close, share, got)
    last = [shift("y", side, i + 1, passed[i]) for i in range(3)] + [
        shift("x", side, i + 1, passed[3 + i]) for i in range(3)
    ]
    home = pool_near(own_source, 1, place, requests, wide, samples)
    features, hot_grad = finish(home, passed[3], last, hot_own, hot_got)
    return (features, hot_grad)


def solution(mesh):
    fine = Mesh(mesh.devices.reshape(4, 4, 8, 2), ALL)
    every = P(ALL, None)
    return jax.shard_map(
        shards,
        mesh=fine,
        in_specs=(P(("y", "x"), None), every, every, every, P(), every, every, every),
        out_specs=(every, P(("z", "core"), None)),
        check_vma=False,
    )
```

```python
import functools

import jax
import jax.numpy as jnp
from jax import lax
from jax.experimental import pallas as pl
from jax.experimental.pallas import tpu as pltpu
from jax.sharding import Mesh, PartitionSpec as P

cold_scale = 0.03125
hot_scale = 0.0625
CHUNK = 128
PAD = 8
ALL = ("y", "x", "z", "core")


def widen_kernel(table_hbm, wide_ref, buf, sem):
    steps = sem.shape[0]
    rows = buf.shape[0] // steps

    def fetch(step):
        part = pl.ds(step * rows, rows)
        return pltpu.make_async_copy(table_hbm.at[part], buf.at[part], sem.at[step])

    for step in range(steps):
        fetch(step).start()
    edge = jnp.zeros((PAD, wide_ref.shape[1]), jnp.float32)
    wide_ref[:PAD] = edge
    wide_ref[wide_ref.shape[0] - PAD :] = edge
    for step in range(steps):
        fetch(step).wait()
        part = slice(step * rows, (step + 1) * rows)
        wide_ref[PAD + step * rows : PAD + (step + 1) * rows] = buf[part].astype(jnp.float32)


def widen(table):
    rows, width = table.shape
    return pl.pallas_call(
        widen_kernel,
        in_specs=[pl.BlockSpec(memory_space=pl.ANY)],
        out_specs=pl.BlockSpec(memory_space=pltpu.VMEM),
        out_shape=pltpu.VMEM((rows + 2 * PAD, width), jnp.float32),
        scratch_shapes=[
            pltpu.VMEM((rows, width), jnp.bfloat16),
            pltpu.SemaphoreType.DMA((16,)),
        ],
        compiler_params=pltpu.CompilerParams(vmem_limit_bytes=44 << 20),
        cost_estimate=pl.CostEstimate(
            flops=rows * width, bytes_accessed=rows * width * 6, transcendentals=0
        ),
        name="widen",
    )(table)


def pack_kernel(a, b, c, out):
    for part, ref in enumerate((a, b, c)):
        for bucket in range(ref.shape[0]):
            out[bucket, part : part + 1, :] = ref[bucket : bucket + 1, :]


def pack(parts):
    buckets, slots = parts[0].shape
    return pl.pallas_call(
        pack_kernel,
        grid=(1,),
        in_specs=[pl.BlockSpec((buckets, slots), lambda i: (0, 0))] * 3,
        out_specs=pl.BlockSpec((buckets, 3, slots), lambda i: (0, 0, 0)),
        out_shape=jax.ShapeDtypeStruct((buckets, 3, slots), jnp.int32),
        compiler_params=pltpu.CompilerParams(vmem_limit_bytes=60 << 20),
        cost_estimate=pl.CostEstimate(
            flops=0, bytes_accessed=buckets * slots * 24, transcendentals=0
        ),
        name="pack",
    )(*parts)


def pool_task(rows_ref, slots_ref, wide_ref, acc, bufs):
    slots = rows_ref.shape[2]
    samples, width = acc.shape
    sublane = lax.broadcasted_iota(jnp.int32, (PAD, width), 0)

    def gather(chunk):
        buf = bufs[chunk % 2]
        for tile in range(CHUNK // PAD):
            merged = None
            for lane in range(PAD):
                row = rows_ref[0, 0, chunk * CHUNK + tile * PAD + lane]
                near = wide_ref[pl.ds(row + (PAD - lane), PAD), :]
                merged = near if lane == 0 else jnp.where(sublane == lane, near, merged)
            buf[tile * PAD : (tile + 1) * PAD, :] = merged

    def pool(chunk):
        cols = slice(chunk * CHUNK, (chunk + 1) * CHUNK)
        ids = lax.broadcasted_iota(jnp.int32, (samples, CHUNK), 0)
        weight = slots_ref[0, 2:3, cols].astype(jnp.float32) * cold_scale
        weights = jnp.where(ids == slots_ref[0, 1:2, cols], weight, 0.0).astype(jnp.bfloat16)
        part = jnp.dot(
            weights,
            bufs[chunk % 2][...].astype(jnp.bfloat16),
            preferred_element_type=jnp.float32,
        )
        if chunk == 0:
            acc[...] = part
        else:
            acc[...] += part

    gather(0)
    for chunk in range(slots // CHUNK):
        if (chunk + 1) * CHUNK < slots:
            gather(chunk + 1)
        pool(chunk)


def routes():
    found = {}
    for dx in (1, 2, 3):
        for dy in (1, 2, 3):
            if dx == 2 and dy == 2:
                moves = [(1, 0, 0, 2), (4, 0, 2, 2)]
            elif dx == 2:
                moves = [(2 + dy, 2, 0, 4)]
            elif dy == 2:
                moves = [(dx - 1, 2, 0, 4)]
            else:
                moves = [(dx - 1, 3 * (dy - 1), 0, 2), (2 + dy, 3 * (dx - 1), 2, 2)]
            found[dy, dx] = moves
    return found


ROUTES = routes()
BLOCKS = (9, 3, 9, 9, 3, 9)


def far_kernel(place, rows_ref, slots_ref, wide_ref, *refs):
    del place
    outs, (acc, buf0, buf1) = refs[:6], refs[6:]
    pool_task(rows_ref, slots_ref, wide_ref, acc, (buf0, buf1))
    task = pl.program_id(0)
    part = acc.shape[0] // 4
    for (dy, dx), moves in ROUTES.items():

        @pl.when(task == 3 * (dx - 1) + dy - 1)
        def _():
            for index, to, first, count in moves:
                for unit in range(count):
                    start = (first + unit) * part
                    outs[index][to + unit] = acc[start : start + part]


def near_kernel(place, rows_ref, slots_ref, wide_ref, out, acc, buf0, buf1):
    del place
    pool_task(rows_ref, slots_ref, wide_ref, acc, (buf0, buf1))
    out[0] = acc[...]


def source(place, dy, dx):
    return ((place[2] + dy) & 3) * 4 + ((place[3] + dx) & 3)


def far_source(t, place):
    return source(place, t % 3 + 1, t // 3 + 1)


def near_source(t, place):
    return source(place, jnp.where(t < 3, t + 1, 0), jnp.where(t < 3, 0, t - 2))


def own_source(t, place):
    return source(place, 0, 0)


def pool_call(body, name, origin, tasks, place, requests, wide, samples, out_specs, out_shape):
    _, parts, slots = requests.shape
    width = wide.shape[1]

    def spec(space):
        return pl.BlockSpec(
            (1, parts, slots), lambda t, place: (origin(t, place), 0, 0), memory_space=space
        )

    return pl.pallas_call(
        body,
        grid_spec=pltpu.PrefetchScalarGridSpec(
            num_scalar_prefetch=1,
            grid=(tasks,),
            in_specs=[spec(pltpu.SMEM), spec(pltpu.VMEM), pl.BlockSpec(memory_space=pltpu.VMEM)],
            out_specs=out_specs,
            scratch_shapes=[pltpu.VMEM((samples, width), jnp.float32)]
            + [pltpu.VMEM((CHUNK, width), jnp.float32)] * 2,
        ),
        out_shape=out_shape,
        compiler_params=pltpu.CompilerParams(vmem_limit_bytes=20 << 20),
        cost_estimate=pl.CostEstimate(
            flops=tasks * 2 * samples * slots * width,
            bytes_accessed=tasks * slots * width * 20,
            transcendentals=0,
        ),
        name=name,
    )(place, requests, requests, wide)


def pool_far(place, requests, wide, samples):
    width = wide.shape[1]
    specs = [pl.BlockSpec(memory_space=pltpu.VMEM)] * 6
    shape = [pltpu.VMEM((blocks, samples // 4, width), jnp.float32) for blocks in BLOCKS]
    return pool_call(
        far_kernel, "pool_far", far_source, 9, place, requests, wide, samples, specs, shape
    )


def pool_near(name, origin, tasks, place, requests, wide, samples):
    width = wide.shape[1]
    return pool_call(
        near_kernel,
        name,
        origin,
        tasks,
        place,
        requests,
        wide,
        samples,
        pl.BlockSpec((1, samples, width), lambda t, place: (t, 0, 0)),
        jax.ShapeDtypeStruct((tasks, samples, width), jnp.float32),
    )


def attach_kernel(*refs):
    parts, outs, share_ref = refs[:8], refs[14:20], refs[20]
    p = [ref[...] for ref in parts]
    share = ((p[0] + p[1]) + (p[2] + p[3])) + ((p[4] + p[5]) + (p[6] + p[7]))
    share_ref[...] = share
    half = share.shape[0] // 2
    for out in outs[:3]:
        out[0] = share[:half]
    for out in outs[3:]:
        out[0] = share[half:]


def attach(parts, sent):
    block, width = parts[0].shape
    last = [
        pl.BlockSpec((1, block // 2, width), lambda i, end=blocks - 1: (end, 0, 0))
        for blocks in BLOCKS
    ]
    whole = pl.BlockSpec((block, width), lambda i: (0, 0))
    return pl.pallas_call(
        attach_kernel,
        grid=(1,),
        in_specs=[whole] * 8 + [pl.BlockSpec(memory_space=pl.ANY)] * 6,
        out_specs=last + [whole],
        out_shape=[jax.ShapeDtypeStruct(each.shape, jnp.float32) for each in sent]
        + [jax.ShapeDtypeStruct((block, width), jnp.float32)],
        input_output_aliases={8 + i: i for i in range(6)},
        compiler_params=pltpu.CompilerParams(vmem_limit_bytes=8 << 20),
        cost_estimate=pl.CostEstimate(
            flops=block * width * 8, bytes_accessed=block * width * 48, transcendentals=0
        ),
        name="attach",
    )(*parts, *sent)


def relay_kernel(near_ref, share_ref, *refs):
    got, outs = refs[:6], refs[6:]
    samples = near_ref.shape[1]
    part = samples // 4
    terms = {}
    for (dy, dx), moves in ROUTES.items():
        for index, to, first, count in moves:
            out = dy - 1 if index < 3 else 2 + dx
            for unit in range(count):
                terms.setdefault((out, first + unit), []).append((index, to + unit))
    for out in range(6):
        for unit in range(4):
            rows = slice(unit * part, (unit + 1) * part)
            total = near_ref[out, rows]
            for index, block in terms.get((out, unit), ()):
                total = total + got[index][block]
            outs[out][rows] = total
    for s in range(2):
        one, two, three = (got[3 * s + i][BLOCKS[3 * s + i] - 1] for i in range(3))
        share = (share_ref[s * part : (s + 1) * part] + two) + (one + three)
        for i in range(3):
            outs[3 * s + i][samples:] = share


def relay(near, share, got):
    _, samples, width = near.shape
    tall = samples + share.shape[0] // 2
    return pl.pallas_call(
        relay_kernel,
        out_shape=[jax.ShapeDtypeStruct((tall, width), jnp.float32)] * 6,
        compiler_params=pltpu.CompilerParams(vmem_limit_bytes=16 << 20),
        cost_estimate=pl.CostEstimate(
            flops=samples * width * 12, bytes_accessed=samples * width * 84, transcendentals=0
        ),
        name="relay",
    )(near, share, *got)


def finish_kernel(near_ref, mine0, mine1, a, b, c, d, e, f, hot_own, hot_got, out, grad):
    samples, width = hot_own.shape
    half = grad.shape[0] // 2
    cold = near_ref[0] + (
        (a[:samples] + b[:samples] + c[:samples]) + (d[:samples] + e[:samples] + f[:samples])
    )
    out[:, :width] = cold.astype(jnp.bfloat16)
    out[:, width:] = (hot_own[...] + hot_got[...]).astype(jnp.bfloat16)
    grad[:half] = (mine0[samples:] + b[samples:]) + (a[samples:] + c[samples:])
    grad[half:] = (mine1[samples:] + e[samples:]) + (d[samples:] + f[samples:])


def finish(near, mine0, mine1, got, hot_own, hot_got):
    _, samples, width = near.shape
    tall = mine0.shape[0]
    whole = pl.BlockSpec((samples, width), lambda i: (0, 0))
    more = pl.BlockSpec((tall, width), lambda i: (0, 0))
    share = 2 * (tall - samples)
    return pl.pallas_call(
        finish_kernel,
        grid=(1,),
        in_specs=[pl.BlockSpec((1, samples, width), lambda i: (0, 0, 0))]
        + [more] * 8
        + [whole] * 2,
        out_specs=[
            pl.BlockSpec((samples, 2 * width), lambda i: (0, 0)),
            pl.BlockSpec((share, width), lambda i: (0, 0)),
        ],
        out_shape=[
            jax.ShapeDtypeStruct((samples, 2 * width), jnp.bfloat16),
            jax.ShapeDtypeStruct((share, width), jnp.float32),
        ],
        compiler_params=pltpu.CompilerParams(vmem_limit_bytes=16 << 20),
        cost_estimate=pl.CostEstimate(
            flops=samples * width * 8, bytes_accessed=samples * width * 40, transcendentals=0
        ),
        name="finish",
    )(near, mine0, mine1, *got, hot_own, hot_got)


def hot_kernel(place, idx0, idx1, cnt0, cnt1, cot0, cot1, table_ref, *refs):
    grads, (own_ref, other_ref, inc, pooled, held) = refs[:8], refs[8:]
    block = table_ref.shape[1]
    lookups, samples = idx0.shape
    depth = held.shape[0]
    lanes = 128
    tile = 16

    def step(ahead, carry):
        blk = 2 * lax.rem(place[0] + ahead, depth) + place[1]
        start = blk * block
        for lane in range(2 * samples // lanes):
            idx_ref, cnt_ref = (idx0, cnt0) if lane * lanes < samples else (idx1, cnt1)
            first = lane * lanes % samples
            cols = slice(first, first + lanes)
            to = slice(lane * lanes, (lane + 1) * lanes)
            local = jnp.clip(idx_ref[:, cols] - start, -1, block)
            weight = cnt_ref[:, cols].astype(jnp.float32) * hot_scale
            keys = []
            for k in range(lookups):
                keys.append(
                    (
                        jnp.broadcast_to(local[k : k + 1], (tile, lanes)).astype(jnp.int16),
                        jnp.broadcast_to(weight[k : k + 1], (tile, lanes)).astype(jnp.bfloat16),
                    )
                )
            base = lax.broadcasted_iota(jnp.int32, (tile, lanes), 0)
            for group in range(block // tile):
                ids = (base + group * tile).astype(jnp.int16)
                total = jnp.zeros((tile, lanes), jnp.bfloat16)
                for key, value in keys:
                    total = total + jnp.where(ids == key, value, jnp.bfloat16(0))
                inc[group * tile : (group + 1) * tile, to] = total
        held[ahead] = jnp.dot(
            inc[:, :samples], cot0[...], preferred_element_type=jnp.float32
        ) + jnp.dot(inc[:, samples:], cot1[...], preferred_element_type=jnp.float32)
        part = lax.dot_general(
            table_ref[blk],
            inc[...],
            (((0,), (0,)), ((), ())),
            preferred_element_type=jnp.float32,
        )

        @pl.when(ahead == 0)
        def _():
            pooled[...] = part

        @pl.when(ahead > 0)
        def _():
            pooled[...] += part

        return carry

    lax.fori_loop(0, depth, step, 0)
    own_ref[...] = jnp.transpose(pooled[:, :samples])
    other_ref[...] = jnp.transpose(pooled[:, samples:])
    for ahead in range(depth):
        grads[ahead][...] = held[ahead]


def hot_call(place, pairs, table, depth):
    blocks, block, width = table.shape
    lookups, samples = pairs[0].shape

    def whole(*shape):
        return pl.BlockSpec(shape, lambda i, place: (0,) * len(shape))

    return pl.pallas_call(
        hot_kernel,
        grid_spec=pltpu.PrefetchScalarGridSpec(
            num_scalar_prefetch=1,
            grid=(1,),
            in_specs=[whole(lookups, samples)] * 4
            + [whole(samples, width)] * 2
            + [whole(blocks, block, width)],
            out_specs=[whole(block, width)] * depth + [whole(samples, width)] * 2,
            scratch_shapes=[
                pltpu.VMEM((block, 2 * samples), jnp.bfloat16),
                pltpu.VMEM((width, 2 * samples), jnp.float32),
                pltpu.VMEM((depth, block, width), jnp.float32),
            ],
        ),
        out_shape=[jax.ShapeDtypeStruct((block, width), jnp.float32)] * depth
        + [jax.ShapeDtypeStruct((samples, width), jnp.float32)] * 2,
        compiler_params=pltpu.CompilerParams(vmem_limit_bytes=60 << 20),
        cost_estimate=pl.CostEstimate(
            flops=8 * samples * depth * block * width,
            bytes_accessed=2 * samples * depth * block * 16,
            transcendentals=0,
        ),
        name="hot",
    )(place, *pairs, table)


def shift(axis, size, by, value):
    return lax.ppermute(value, axis, [(i, (i + by) % size) for i in range(size)])


def shards(
    cold_table, slot_row, slot_sample, slot_count, hot_table, hot_index, hot_count, hot_cotangent
):
    samples = hot_index.shape[0]
    width = cold_table.shape[1]
    side = lax.axis_size("x")
    depth = lax.axis_size("z")
    y, x, z, core = (lax.axis_index(axis) for axis in ALL)
    place = jnp.stack([z, core, y, x])

    asked = pack([slot_row, slot_sample, slot_count])
    requests = lax.all_to_all(asked, ("y", "x"), split_axis=0, concat_axis=0, tiled=True)

    pairs = []
    for value in (hot_index.T, hot_count.T, hot_cotangent):
        pairs += [value, shift("core", 2, 1, value)]
    blocks = hot_table.reshape(2 * depth, -1, width)
    *grads, hot_own, hot_other = hot_call(place, pairs, blocks, depth)
    hot_got = shift("core", 2, 1, hot_other)
    parts = [grads[0]] + [shift("z", depth, by, grads[by]) for by in range(1, depth)]

    cold_table, requests, hot_got, place = lax.optimization_barrier(
        (cold_table, requests, hot_got, place)
    )
    wide = widen(cold_table)
    sent = pool_far(place, requests, wide, samples)
    *sent, share = attach(parts, sent)
    got = [shift("x", side, i + 1, sent[i]) for i in range(3)] + [
        shift("y", side, i + 1, sent[3 + i]) for i in range(3)
    ]
    close = pool_near("pool_near", near_source, 6, place, requests, wide, samples)
    passed = relay(close, share, got)
    last = [shift("y", side, i + 1, passed[i]) for i in range(3)] + [
        shift("x", side, i + 1, passed[3 + i]) for i in range(3)
    ]
    home = pool_near("pool_own", own_source, 1, place, requests, wide, samples)
    features, hot_grad = finish(home, passed[0], passed[3], last, hot_own, hot_got)
    return (features, hot_grad)


def solution(mesh):
    fine = Mesh(mesh.devices.reshape(4, 4, 8, 2), ALL)
    every = P(ALL, None)
    return jax.shard_map(
        shards,
        mesh=fine,
        in_specs=(P(("y", "x"), None), every, every, every, P(), every, every, every),
        out_specs=(every, P(("z", "core"), None)),
        check_vma=False,
    )
```

```python
import functools

import jax
import jax.numpy as jnp
from jax import lax
from jax.experimental import pallas as pl
from jax.experimental.pallas import tpu as pltpu
from jax.sharding import Mesh, PartitionSpec as P

cold_scale = 0.03125
hot_scale = 0.0625
CHUNK = 128
PAD = 8
ALL = ("y", "x", "z", "core")


def widen_kernel(table_hbm, wide_ref, buf, sem):
    steps = sem.shape[0]
    rows = buf.shape[0] // steps

    def fetch(step):
        part = pl.ds(step * rows, rows)
        return pltpu.make_async_copy(table_hbm.at[part], buf.at[part], sem.at[step])

    for step in range(steps):
        fetch(step).start()
    edge = jnp.zeros((PAD, wide_ref.shape[1]), jnp.float32)
    wide_ref[:PAD] = edge
    wide_ref[wide_ref.shape[0] - PAD :] = edge
    for step in range(steps):
        fetch(step).wait()
        part = slice(step * rows, (step + 1) * rows)
        wide_ref[PAD + step * rows : PAD + (step + 1) * rows] = buf[part].astype(jnp.float32)


def widen(table):
    rows, width = table.shape
    return pl.pallas_call(
        widen_kernel,
        in_specs=[pl.BlockSpec(memory_space=pl.ANY)],
        out_specs=pl.BlockSpec(memory_space=pltpu.VMEM),
        out_shape=pltpu.VMEM((rows + 2 * PAD, width), jnp.float32),
        scratch_shapes=[
            pltpu.VMEM((rows, width), jnp.bfloat16),
            pltpu.SemaphoreType.DMA((16,)),
        ],
        compiler_params=pltpu.CompilerParams(vmem_limit_bytes=44 << 20),
        cost_estimate=pl.CostEstimate(
            flops=rows * width, bytes_accessed=rows * width * 6, transcendentals=0
        ),
        name="widen",
    )(table)


def pack_kernel(a, b, c, out):
    for part, ref in enumerate((a, b, c)):
        for bucket in range(ref.shape[0]):
            out[bucket, part : part + 1, :] = ref[bucket : bucket + 1, :]


def pack(parts):
    buckets, slots = parts[0].shape
    return pl.pallas_call(
        pack_kernel,
        grid=(1,),
        in_specs=[pl.BlockSpec((buckets, slots), lambda i: (0, 0))] * 3,
        out_specs=pl.BlockSpec((buckets, 3, slots), lambda i: (0, 0, 0)),
        out_shape=jax.ShapeDtypeStruct((buckets, 3, slots), jnp.int32),
        compiler_params=pltpu.CompilerParams(vmem_limit_bytes=60 << 20),
        cost_estimate=pl.CostEstimate(
            flops=0, bytes_accessed=buckets * slots * 24, transcendentals=0
        ),
        name="pack",
    )(*parts)


def pool_task(rows_ref, slots_ref, wide_ref, acc, bufs):
    slots = rows_ref.shape[2]
    samples, width = acc.shape
    sublane = lax.broadcasted_iota(jnp.int32, (PAD, width), 0)

    def gather(chunk):
        buf = bufs[chunk % 2]
        for tile in range(CHUNK // PAD):
            merged = None
            for lane in range(PAD):
                row = rows_ref[0, 0, chunk * CHUNK + tile * PAD + lane]
                near = wide_ref[pl.ds(row + (PAD - lane), PAD), :]
                merged = near if lane == 0 else jnp.where(sublane == lane, near, merged)
            buf[tile * PAD : (tile + 1) * PAD, :] = merged

    def pool(chunk):
        cols = slice(chunk * CHUNK, (chunk + 1) * CHUNK)
        ids = lax.broadcasted_iota(jnp.int32, (samples, CHUNK), 0)
        weight = slots_ref[0, 2:3, cols].astype(jnp.float32) * cold_scale
        weights = jnp.where(ids == slots_ref[0, 1:2, cols], weight, 0.0).astype(jnp.bfloat16)
        part = jnp.dot(
            weights,
            bufs[chunk % 2][...].astype(jnp.bfloat16),
            preferred_element_type=jnp.float32,
        )
        if chunk == 0:
            acc[...] = part
        else:
            acc[...] += part

    gather(0)
    for chunk in range(slots // CHUNK):
        if (chunk + 1) * CHUNK < slots:
            gather(chunk + 1)
        pool(chunk)


def routes():
    found = {}
    for dx in (1, 2, 3):
        for dy in (1, 2, 3):
            if dx == 2 and dy == 2:
                moves = [(1, 0, 0, 2), (4, 0, 2, 2)]
            elif dx == 2:
                moves = [(2 + dy, 2, 0, 4)]
            elif dy == 2:
                moves = [(dx - 1, 2, 0, 4)]
            else:
                moves = [(dx - 1, 3 * (dy - 1), 0, 2), (2 + dy, 3 * (dx - 1), 2, 2)]
            found[dy, dx] = moves
    return found


ROUTES = routes()
BLOCKS = (9, 3, 9, 9, 3, 9)


def far_kernel(place, rows_ref, slots_ref, wide_ref, *refs):
    del place
    outs, (acc, buf0, buf1) = refs[:6], refs[6:]
    pool_task(rows_ref, slots_ref, wide_ref, acc, (buf0, buf1))
    task = pl.program_id(0)
    part = acc.shape[0] // 4
    for (dy, dx), moves in ROUTES.items():

        @pl.when(task == 3 * (dx - 1) + dy - 1)
        def _():
            for index, to, first, count in moves:
                for unit in range(count):
                    start = (first + unit) * part
                    outs[index][to + unit] = acc[start : start + part]


def near_kernel(place, rows_ref, slots_ref, wide_ref, out, acc, buf0, buf1):
    del place
    pool_task(rows_ref, slots_ref, wide_ref, acc, (buf0, buf1))
    out[0] = acc[...]


def source(place, dy, dx):
    return ((place[2] + dy) & 3) * 4 + ((place[3] + dx) & 3)


def far_source(t, place):
    return source(place, t % 3 + 1, t // 3 + 1)


def near_source(t, place):
    return source(place, jnp.where(t < 3, t + 1, 0), jnp.where(t < 3, 0, t - 2))


def own_source(t, place):
    return source(place, 0, 0)


def pool_call(body, name, origin, tasks, place, requests, wide, samples, out_specs, out_shape):
    _, parts, slots = requests.shape
    width = wide.shape[1]

    def spec(space):
        return pl.BlockSpec(
            (1, parts, slots), lambda t, place: (origin(t, place), 0, 0), memory_space=space
        )

    return pl.pallas_call(
        body,
        grid_spec=pltpu.PrefetchScalarGridSpec(
            num_scalar_prefetch=1,
            grid=(tasks,),
            in_specs=[spec(pltpu.SMEM), spec(pltpu.VMEM), pl.BlockSpec(memory_space=pltpu.VMEM)],
            out_specs=out_specs,
            scratch_shapes=[pltpu.VMEM((samples, width), jnp.float32)]
            + [pltpu.VMEM((CHUNK, width), jnp.float32)] * 2,
        ),
        out_shape=out_shape,
        compiler_params=pltpu.CompilerParams(vmem_limit_bytes=20 << 20),
        cost_estimate=pl.CostEstimate(
            flops=tasks * 2 * samples * slots * width,
            bytes_accessed=tasks * slots * width * 20,
            transcendentals=0,
        ),
        name=name,
    )(place, requests, requests, wide)


def pool_far(place, requests, wide, samples):
    width = wide.shape[1]
    specs = [pl.BlockSpec(memory_space=pltpu.VMEM)] * 6
    shape = [pltpu.VMEM((blocks, samples // 4, width), jnp.float32) for blocks in BLOCKS]
    return pool_call(
        far_kernel, "pool_far", far_source, 9, place, requests, wide, samples, specs, shape
    )


def pool_near(name, origin, tasks, place, requests, wide, samples):
    width = wide.shape[1]
    return pool_call(
        near_kernel,
        name,
        origin,
        tasks,
        place,
        requests,
        wide,
        samples,
        pl.BlockSpec((1, samples, width), lambda t, place: (t, 0, 0)),
        jax.ShapeDtypeStruct((tasks, samples, width), jnp.float32),
    )


def attach_kernel(*refs):
    parts, outs, share_ref = refs[:8], refs[14:20], refs[20]
    p = [ref[...] for ref in parts]
    share = ((p[0] + p[1]) + (p[2] + p[3])) + ((p[4] + p[5]) + (p[6] + p[7]))
    share_ref[...] = share
    half = share.shape[0] // 2
    for out in outs[:3]:
        out[0] = share[:half]
    for out in outs[3:]:
        out[0] = share[half:]


def attach(parts, sent):
    block, width = parts[0].shape
    last = [
        pl.BlockSpec((1, block // 2, width), lambda i, end=blocks - 1: (end, 0, 0))
        for blocks in BLOCKS
    ]
    whole = pl.BlockSpec((block, width), lambda i: (0, 0))
    return pl.pallas_call(
        attach_kernel,
        grid=(1,),
        in_specs=[whole] * 8 + [pl.BlockSpec(memory_space=pl.ANY)] * 6,
        out_specs=last + [whole],
        out_shape=[jax.ShapeDtypeStruct(each.shape, jnp.float32) for each in sent]
        + [jax.ShapeDtypeStruct((block, width), jnp.float32)],
        input_output_aliases={8 + i: i for i in range(6)},
        compiler_params=pltpu.CompilerParams(vmem_limit_bytes=8 << 20),
        cost_estimate=pl.CostEstimate(
            flops=block * width * 8, bytes_accessed=block * width * 48, transcendentals=0
        ),
        name="attach",
    )(*parts, *sent)


def relay_kernel(near_ref, share_ref, *refs):
    got, outs = refs[:6], refs[6:]
    samples = near_ref.shape[1]
    part = samples // 4
    terms = {}
    for (dy, dx), moves in ROUTES.items():
        for index, to, first, count in moves:
            out = dy - 1 if index < 3 else 2 + dx
            for unit in range(count):
                terms.setdefault((out, first + unit), []).append((index, to + unit))
    for out in range(6):
        for unit in range(4):
            rows = slice(unit * part, (unit + 1) * part)
            total = near_ref[out, rows]
            for index, block in terms.get((out, unit), ()):
                total = total + got[index][block]
            outs[out][rows] = total
    for s in range(2):
        one, two, three = (got[3 * s + i][BLOCKS[3 * s + i] - 1] for i in range(3))
        share = (share_ref[s * part : (s + 1) * part] + two) + (one + three)
        for i in range(3):
            outs[3 * s + i][samples:] = share


def relay(near, share, got):
    _, samples, width = near.shape
    tall = samples + share.shape[0] // 2
    return pl.pallas_call(
        relay_kernel,
        out_shape=[jax.ShapeDtypeStruct((tall, width), jnp.float32)] * 6,
        compiler_params=pltpu.CompilerParams(vmem_limit_bytes=16 << 20),
        cost_estimate=pl.CostEstimate(
            flops=samples * width * 12, bytes_accessed=samples * width * 84, transcendentals=0
        ),
        name="relay",
    )(near, share, *got)


def finish_kernel(near_ref, mine0, mine1, a, b, c, d, e, f, hot_own, hot_got, out, grad):
    samples, width = hot_own.shape
    half = grad.shape[0] // 2
    cold = near_ref[0] + (
        (a[:samples] + b[:samples] + c[:samples]) + (d[:samples] + e[:samples] + f[:samples])
    )
    out[:, :width] = cold.astype(jnp.bfloat16)
    out[:, width:] = (hot_own[...] + hot_got[...]).astype(jnp.bfloat16)
    grad[:half] = (mine0[samples:] + b[samples:]) + (a[samples:] + c[samples:])
    grad[half:] = (mine1[samples:] + e[samples:]) + (d[samples:] + f[samples:])


def finish(near, mine0, mine1, got, hot_own, hot_got):
    _, samples, width = near.shape
    tall = mine0.shape[0]
    whole = pl.BlockSpec((samples, width), lambda i: (0, 0))
    more = pl.BlockSpec((tall, width), lambda i: (0, 0))
    share = 2 * (tall - samples)
    return pl.pallas_call(
        finish_kernel,
        grid=(1,),
        in_specs=[pl.BlockSpec((1, samples, width), lambda i: (0, 0, 0))]
        + [more] * 8
        + [whole] * 2,
        out_specs=[
            pl.BlockSpec((samples, 2 * width), lambda i: (0, 0)),
            pl.BlockSpec((share, width), lambda i: (0, 0)),
        ],
        out_shape=[
            jax.ShapeDtypeStruct((samples, 2 * width), jnp.bfloat16),
            jax.ShapeDtypeStruct((share, width), jnp.float32),
        ],
        compiler_params=pltpu.CompilerParams(vmem_limit_bytes=16 << 20),
        cost_estimate=pl.CostEstimate(
            flops=samples * width * 8, bytes_accessed=samples * width * 40, transcendentals=0
        ),
        name="finish",
    )(near, mine0, mine1, *got, hot_own, hot_got)


def hot_kernel(place, idx0, idx1, cnt0, cnt1, cot0, cot1, table_ref, *refs):
    grads, (own_ref, other_ref, inc, pooled, held, table, fetched, stored) = refs[:8], refs[8:]
    block = table_ref.shape[1]
    lookups, samples = idx0.shape
    depth = held.shape[0]
    lanes = 128
    tile = 16

    def fetch(ahead):
        blk = 2 * lax.rem(place[0] + ahead, depth) + place[1]
        return pltpu.make_async_copy(table_ref.at[blk], table.at[ahead], fetched.at[ahead])

    def store(ahead):
        return pltpu.make_async_copy(held.at[ahead], grads[ahead], stored.at[ahead])

    for ahead in range(depth):
        fetch(ahead).start()

    def step(ahead, carry):
        blk = 2 * lax.rem(place[0] + ahead, depth) + place[1]
        start = blk * block
        for lane in range(2 * samples // lanes):
            idx_ref, cnt_ref = (idx0, cnt0) if lane * lanes < samples else (idx1, cnt1)
            first = lane * lanes % samples
            cols = slice(first, first + lanes)
            to = slice(lane * lanes, (lane + 1) * lanes)
            local = jnp.clip(idx_ref[:, cols] - start, -1, block)
            weight = cnt_ref[:, cols].astype(jnp.float32) * hot_scale
            keys = []
            for k in range(lookups):
                keys.append(
                    (
                        jnp.broadcast_to(local[k : k + 1], (tile, lanes)).astype(jnp.int16),
                        jnp.broadcast_to(weight[k : k + 1], (tile, lanes)).astype(jnp.bfloat16),
                    )
                )
            base = lax.broadcasted_iota(jnp.int32, (tile, lanes), 0)
            for group in range(block // tile):
                ids = (base + group * tile).astype(jnp.int16)
                total = jnp.zeros((tile, lanes), jnp.bfloat16)
                for key, value in keys:
                    total = total + jnp.where(ids == key, value, jnp.bfloat16(0))
                inc[group * tile : (group + 1) * tile, to] = total
        held[ahead] = jnp.dot(
            inc[:, :samples], cot0[...], preferred_element_type=jnp.float32
        ) + jnp.dot(inc[:, samples:], cot1[...], preferred_element_type=jnp.float32)
        for k in range(depth - 1):

            @pl.when(ahead == k + 1)
            def _():
                store(k).start()

        fetch(ahead).wait()
        part = lax.dot_general(
            table[ahead],
            inc[...],
            (((0,), (0,)), ((), ())),
            preferred_element_type=jnp.float32,
        )

        @pl.when(ahead == 0)
        def _():
            pooled[...] = part

        @pl.when(ahead > 0)
        def _():
            pooled[...] += part

        return carry

    lax.fori_loop(0, depth, step, 0)
    own_ref[...] = jnp.transpose(pooled[:, :samples])
    other_ref[...] = jnp.transpose(pooled[:, samples:])
    store(depth - 1).start()
    for ahead in range(depth):
        store(ahead).wait()


def hot_call(place, pairs, table, depth):
    blocks, block, width = table.shape
    lookups, samples = pairs[0].shape

    def whole(*shape):
        return pl.BlockSpec(shape, lambda i, place: (0,) * len(shape))

    return pl.pallas_call(
        hot_kernel,
        grid_spec=pltpu.PrefetchScalarGridSpec(
            num_scalar_prefetch=1,
            grid=(1,),
            in_specs=[whole(lookups, samples)] * 4
            + [whole(samples, width)] * 2
            + [pl.BlockSpec(memory_space=pl.ANY)],
            out_specs=[pl.BlockSpec(memory_space=pl.ANY)] * depth + [whole(samples, width)] * 2,
            scratch_shapes=[
                pltpu.VMEM((block, 2 * samples), jnp.bfloat16),
                pltpu.VMEM((width, 2 * samples), jnp.float32),
                pltpu.VMEM((depth, block, width), jnp.float32),
                pltpu.VMEM((depth, block, width), jnp.bfloat16),
                pltpu.SemaphoreType.DMA((depth,)),
                pltpu.SemaphoreType.DMA((depth,)),
            ],
        ),
        out_shape=[jax.ShapeDtypeStruct((block, width), jnp.float32)] * depth
        + [jax.ShapeDtypeStruct((samples, width), jnp.float32)] * 2,
        compiler_params=pltpu.CompilerParams(vmem_limit_bytes=60 << 20),
        cost_estimate=pl.CostEstimate(
            flops=8 * samples * depth * block * width,
            bytes_accessed=2 * samples * depth * block * 16,
            transcendentals=0,
        ),
        name="hot",
    )(place, *pairs, table)


def shift(axis, size, by, value):
    return lax.ppermute(value, axis, [(i, (i + by) % size) for i in range(size)])


def shards(
    cold_table, slot_row, slot_sample, slot_count, hot_table, hot_index, hot_count, hot_cotangent
):
    samples = hot_index.shape[0]
    width = cold_table.shape[1]
    side = lax.axis_size("x")
    depth = lax.axis_size("z")
    y, x, z, core = (lax.axis_index(axis) for axis in ALL)
    place = jnp.stack([z, core, y, x])

    asked = pack([slot_row, slot_sample, slot_count])
    requests = lax.all_to_all(asked, ("y", "x"), split_axis=0, concat_axis=0, tiled=True)

    pairs = []
    for value in (hot_index.T, hot_count.T, hot_cotangent):
        pairs += [value, shift("core", 2, 1, value)]
    blocks = hot_table.reshape(2 * depth, -1, width)
    *grads, hot_own, hot_other = hot_call(place, pairs, blocks, depth)
    hot_got = shift("core", 2, 1, hot_other)
    parts = [grads[0]] + [shift("z", depth, by, grads[by]) for by in range(1, depth)]

    cold_table, requests, hot_got, place = lax.optimization_barrier(
        (cold_table, requests, hot_got, place)
    )
    wide = widen(cold_table)
    sent = pool_far(place, requests, wide, samples)
    *sent, share = attach(parts, sent)
    got = [shift("x", side, i + 1, sent[i]) for i in range(3)] + [
        shift("y", side, i + 1, sent[3 + i]) for i in range(3)
    ]
    close = pool_near("pool_near", near_source, 6, place, requests, wide, samples)
    passed = relay(close, share, got)
    last = [shift("y", side, i + 1, passed[i]) for i in range(3)] + [
        shift("x", side, i + 1, passed[3 + i]) for i in range(3)
    ]
    home = pool_near("pool_own", own_source, 1, place, requests, wide, samples)
    features, hot_grad = finish(home, passed[0], passed[3], last, hot_own, hot_got)
    return (features, hot_grad)


def solution(mesh):
    fine = Mesh(mesh.devices.reshape(4, 4, 8, 2), ALL)
    every = P(ALL, None)
    return jax.shard_map(
        shards,
        mesh=fine,
        in_specs=(P(("y", "x"), None), every, every, every, P(), every, every, every),
        out_specs=(every, P(("z", "core"), None)),
        check_vma=False,
    )
```
